128 devices in a mesh: fsdp: 16 (over x, z), dp: 8 (over y, core).
Axes of the slice: x: 4, y: 4, z: 4, core: 2. Of those that a mesh axis runs over, the one named last changes fastest.
Arguments:
- grad_parts: bfloat16 [8, 16384, 2048], P('dp', 'fsdp'), may hold values from -6 to 6
- old_master: float32 [16384, 2048], P(('fsdp', 'dp')), may hold values from -0.25 to 0.25
- old_mean: bfloat16 [16384, 2048], P(('fsdp', 'dp')), may hold values from -1 to 1
- old_mean_scale: bfloat16 [16384], P(('fsdp', 'dp')), may hold values from 0.049804688 to 0.5
- old_square: bfloat16 [16384, 2048], P(('fsdp', 'dp')), may hold values from 0.049804688 to 1
- old_square_scale: bfloat16 [16384], P(('fsdp', 'dp')), may hold values from 0.29882812 to 3
- old_map: int32 [16384], replicated, may hold values from 0 to 16383, as said below
Outputs:
- weights: bfloat16 [16384, 2048], P('fsdp')
- master: float32 [16384, 2048], P(('fsdp', 'dp'))
- mean_codes: bfloat16 [16384, 2048], P(('fsdp', 'dp'))
- mean_scales: bfloat16 [16384], P(('fsdp', 'dp'))
- square_codes: bfloat16 [16384, 2048], P(('fsdp', 'dp'))
- square_scales: bfloat16 [16384], P(('fsdp', 'dp'))
The draws below stay inside these ranges and needn't reach their ends.
Inputs may be any that keep to these rules, and one draw needn't show every extreme that they name: old_map is a permutation of the old slots; old slot s lies on device s // 128 counted along fsdp+dp with fsdp major, and block b belongs to new owner b // 128 counted the same way. Every device holds exactly 128 old slots; one device holds at most 2 blocks of one new owner, and every draw has a pair with exactly 2.
All inputs are finite; a program needn't handle non-finite values. Where the reference program divides by a largest or mean magnitude, that divisor is 1e-20 or more.
Results may differ from the reference program's by a relative error of at most 0.02.
Values may be sent and summed in bfloat16 or wider, within the bound.
No kernel may reach another device: no remote copies, remote signals or barrier semaphores. Data moves between devices by JAX's collectives and lax.ppermute only.
A program may use at most 64 MiB of HBM per device.

```python
import math
import jax
import jax.numpy as jnp
from jax import lax

BLOCK = 2048
BLK_DEV = 128
NB = 16384
MOST = 2
N_DP = 8
DEVICES = 128


def draw_old_master(key, part):
    key_rough = jax.random.fold_in(key, 21)
    rough = jax.random.normal(key_rough, (NB, BLOCK), jnp.float32)
    values = jnp.clip(0.03 * rough, -0.12, 0.12)
    return values.astype(jnp.float32)


def draw_old_map(key, part):
    key_slots = jax.random.fold_in(key, 11)
    key_order = jax.random.fold_in(key, 13)
    slot_count = DEVICES * MOST
    slot_ids = jnp.arange(slot_count, dtype=jnp.int32)
    scores = jax.random.randint(key_slots, (slot_count,), 0, slot_count, dtype=jnp.int32) * slot_count + slot_ids
    forced = (slot_ids < MOST) | (slot_ids == MOST) | (slot_ids == MOST * (DEVICES - 1)) | (slot_ids == MOST * (DEVICES // 2))
    scores = jnp.where(forced, slot_ids - slot_count, scores)
    chosen = jnp.argsort(scores, stable=True)[:BLK_DEV].astype(jnp.int32)
    offsets = chosen // MOST
    owners = jnp.arange(DEVICES, dtype=jnp.int32)[:, None]
    senders = (owners + offsets[None, :]) % DEVICES
    ranks = jax.random.randint(key_order, (DEVICES, BLK_DEV), 0, 1048576, dtype=jnp.int32) * BLK_DEV
    ranks = ranks + jnp.arange(BLK_DEV, dtype=jnp.int32)[None, :]
    positions = jnp.argsort(jnp.argsort(ranks, axis=1, stable=True), axis=1, stable=True).astype(jnp.int32)
    columns = jnp.broadcast_to(jnp.arange(BLK_DEV, dtype=jnp.int32)[None, :], (DEVICES, BLK_DEV))
    slot_pos = positions[senders, columns]
    return (senders * BLK_DEV + slot_pos).reshape(-1).astype(jnp.int32)


def level_of(stream_key, shape, shards, least, high):
    gain = 1.0
    for position, blocks in shards:
        draws = jax.random.uniform(jax.random.fold_in(jax.random.fold_in(stream_key, 6), position), (blocks,), jnp.float32, least / len(shards), high / len(shards))
        gain = gain * jnp.repeat(jnp.exp(draws), shape[position] // blocks).reshape((-1,) + (1,) * (len(shape) - 1 - position))
    return gain


def normal_values(key, dims, width, limit, cuts=(), held_as=jnp.bfloat16):
    factor_of = level_of(key, dims, cuts, -0.22, 0.18) if cuts else 1.0
    result = jax.random.normal(key, dims, jnp.float32) * width * factor_of
    return jnp.minimum(jnp.maximum(result, -limit), limit).astype(held_as)


def setup_inputs(seed: int = 0) -> dict:
    streams_of = jax.random.split(jax.random.key(seed), 8)
    grad_parts = normal_values(streams_of[0], (N_DP, NB, BLOCK), 0.4, 6.0, ((0, 8), (1, 16)))
    old_master = draw_old_master(jax.random.fold_in(streams_of[7], 71), 0)
    old_mean = jnp.clip(jax.random.uniform(streams_of[2], (NB, BLOCK), jnp.float32, -1.0, 1.0) * level_of(streams_of[2], (NB, BLOCK), ((0, 128),), -0.4, 0.0), -1.0, 1.0).astype(jnp.bfloat16)
    old_mean_scale = jnp.clip(jnp.exp(math.log(0.5) - 2.306499 * jax.random.uniform(streams_of[3], (NB,), jnp.float32) ** level_of(streams_of[3], (NB,), ((0, 128),), -0.2, 0.2)), 0.049804688, 0.5).astype(jnp.bfloat16)
    old_square = jnp.clip(0.049804688 + 0.9501953 * jax.random.uniform(streams_of[4], (NB, BLOCK), jnp.float32) ** level_of(streams_of[4], (NB, BLOCK), ((0, 128),), -0.2, 0.2), 0.049804688, 1.0).astype(jnp.bfloat16)
    old_square_scale = jnp.clip(jnp.exp(math.log(3.0) - 2.306499 * jax.random.uniform(streams_of[5], (NB,), jnp.float32) ** level_of(streams_of[5], (NB,), ((0, 128),), -0.2, 0.2)), 0.29882812, 3.0).astype(jnp.bfloat16)
    old_map = draw_old_map(jax.random.fold_in(streams_of[7], 71), 0)
    return dict(grad_parts=grad_parts, old_master=old_master, old_mean=old_mean, old_mean_scale=old_mean_scale, old_square=old_square, old_square_scale=old_square_scale, old_map=old_map)


def reference(grad_parts, old_master, old_mean, old_mean_scale, old_square, old_square_scale, old_map):
    gradient = jnp.zeros(grad_parts.shape[1:], jnp.float32)
    for replica in range(N_DP):
        gradient = gradient + grad_parts[replica].astype(jnp.float32)
    weight_old = old_master[old_map]
    mean_old = old_mean[old_map].astype(jnp.float32) * old_mean_scale[old_map].astype(jnp.float32)[:, None]
    square_old = old_square[old_map].astype(jnp.float32) * old_square_scale[old_map].astype(jnp.float32)[:, None]
    mean_next = 0.9 * mean_old + 0.1 * gradient
    square_next = 0.95 * square_old + 0.05 * gradient * gradient
    master = weight_old - 0.05 * (mean_next / (jnp.sqrt(square_next) + 1e-08) + 0.1 * weight_old)
    mean_scales = (lax.optimization_barrier(jnp.max(jnp.abs(mean_next), axis=1)) + 1e-06).astype(jnp.bfloat16)
    square_scales = (lax.optimization_barrier(jnp.max(square_next, axis=1)) + 1e-06).astype(jnp.bfloat16)
    mean_codes = (mean_next / mean_scales.astype(jnp.float32)[:, None]).astype(jnp.bfloat16)
    square_codes = (square_next / square_scales.astype(jnp.float32)[:, None]).astype(jnp.bfloat16)
    weights = master.astype(jnp.bfloat16)
    return (weights, master, mean_codes, mean_scales, square_codes, square_scales)
```

```python
import functools

import jax
import jax.numpy as jnp
from jax import lax
from jax.experimental import pallas as pl
from jax.experimental.pallas import tpu as pltpu
from jax.sharding import PartitionSpec as P

ALL = ("fsdp", "dp")
LANES = 128
SUB = 8


def to_tiles(values):
    rows, cols = values.shape
    tiled = values.reshape(rows // SUB, SUB, cols // LANES, LANES)
    return tiled.transpose(0, 2, 1, 3).reshape(rows * cols // LANES, LANES)


def from_tiles(values, rows, cols):
    tiled = values.reshape(rows // SUB, cols // LANES, SUB, LANES)
    return tiled.transpose(0, 2, 1, 3).reshape(rows, cols)


def pair_rank(owners, keyed):
    matching = owners[:, None] == owners[None, :]
    before = keyed[None, :] < keyed[:, None]
    return jnp.sum(jnp.where(matching & before, 1, 0), axis=1).astype(jnp.int32)


def pack_kernel(rows, chunks, slot_ref, mscale_ref, sscale_ref, master_ref, mean_ref, square_ref, out_ref, wide_mean, wide_square):
    wide_mean[...] = mean_ref[...].astype(jnp.float32)
    wide_square[...] = square_ref[...].astype(jnp.float32)
    for row in range(rows):
        base = (row // SUB) * chunks * SUB + row % SUB
        spots = pl.ds(base, chunks, stride=SUB)
        slot = slot_ref[row]
        out_ref[slot, pl.ds(0, chunks), :] = master_ref[spots, :].astype(jnp.bfloat16)
        out_ref[slot, pl.ds(chunks, chunks), :] = (wide_mean[spots, :] * mscale_ref[row]).astype(jnp.bfloat16)
        out_ref[slot, pl.ds(2 * chunks, chunks), :] = (wide_square[spots, :] * sscale_ref[row]).astype(jnp.bfloat16)


def pack(slots, mean_scale, square_scale, master, mean, square, slot_total):
    rows, cols = master.shape
    chunks = cols // LANES
    smem = pl.BlockSpec(memory_space=pltpu.SMEM)
    vmem = pl.BlockSpec(memory_space=pltpu.VMEM)
    flat = (rows * chunks, LANES)
    return pl.pallas_call(
        functools.partial(pack_kernel, rows, chunks),
        out_shape=jax.ShapeDtypeStruct((slot_total, 3 * chunks, LANES), jnp.bfloat16),
        in_specs=[smem, smem, smem, vmem, vmem, vmem],
        out_specs=vmem,
        scratch_shapes=[pltpu.VMEM(flat, jnp.float32), pltpu.VMEM(flat, jnp.float32)],
        compiler_params=pltpu.CompilerParams(vmem_limit_bytes=24 * 1024 * 1024),
        name="pack",
    )(slots, mean_scale, square_scale, to_tiles(master), to_tiles(mean), to_tiles(square))


def adam_kernel(rows, chunks, slot_ref, in_ref, grad_ref, weights_ref, master_ref, mcode_ref, scode_ref, mscale_ref, sscale_ref, weight_old, mean_old, square_old):
    span = chunks * SUB
    lane = lax.broadcasted_iota(jnp.int32, (SUB, LANES), 1)
    sub = lax.broadcasted_iota(jnp.int32, (SUB, LANES), 0)
    mline = jnp.zeros((SUB, LANES), jnp.float32)
    sline = jnp.zeros((SUB, LANES), jnp.float32)
    for group in range(rows // SUB):
        buf = group % 2
        for r in range(SUB):
            slot = slot_ref[group * SUB + r]
            spots = pl.ds(buf * span + r, chunks, stride=SUB)
            weight_old[spots, :] = in_ref[slot, pl.ds(0, chunks), :].astype(jnp.float32)
            mean_old[spots, :] = in_ref[slot, pl.ds(chunks, chunks), :].astype(jnp.float32)
            square_old[spots, :] = in_ref[slot, pl.ds(2 * chunks, chunks), :].astype(jnp.float32)
        here = pl.ds(buf * span, span)
        there = pl.ds(group * span, span)
        gradient = grad_ref[there, :].astype(jnp.float32)
        old = weight_old[here, :]
        mean_next = 0.9 * mean_old[here, :] + 0.1 * gradient
        square_next = 0.95 * square_old[here, :] + 0.05 * gradient * gradient
        master = old - 0.05 * (mean_next / (jnp.sqrt(square_next) + 1e-08) + 0.1 * old)
        master_ref[there, :] = master
        weights_ref[there, :] = master.astype(jnp.bfloat16)
        mean_next = mean_next.reshape(chunks, SUB, LANES)
        square_next = square_next.reshape(chunks, SUB, LANES)
        mpeak = jnp.max(jnp.max(jnp.abs(mean_next), axis=0), axis=1, keepdims=True)
        speak = jnp.max(jnp.max(square_next, axis=0), axis=1, keepdims=True)
        mscale = (mpeak + 1e-06).astype(jnp.bfloat16).astype(jnp.float32)
        sscale = (speak + 1e-06).astype(jnp.bfloat16).astype(jnp.float32)
        mcode_ref[there, :] = (mean_next * (1.0 / mscale)[None]).reshape(span, LANES).astype(jnp.bfloat16)
        scode_ref[there, :] = (square_next * (1.0 / sscale)[None]).reshape(span, LANES).astype(jnp.bfloat16)
        mine = lane == sub + group * SUB
        mline = jnp.where(mine, mscale, mline)
        sline = jnp.where(mine, sscale, sline)
    mscale_ref[...] = jnp.sum(mline, axis=0, keepdims=True).astype(jnp.bfloat16)
    sscale_ref[...] = jnp.sum(sline, axis=0, keepdims=True).astype(jnp.bfloat16)


def adam(slots, arrived, gradient):
    rows, cols = gradient.shape
    chunks = cols // LANES
    smem = pl.BlockSpec(memory_space=pltpu.SMEM)
    vmem = pl.BlockSpec(memory_space=pltpu.VMEM)
    flat = (rows * chunks, LANES)
    bf16, f32 = jnp.bfloat16, jnp.float32
    stage = pltpu.VMEM((2 * chunks * SUB, LANES), f32)
    outs = pl.pallas_call(
        functools.partial(adam_kernel, rows, chunks),
        out_shape=[
            jax.ShapeDtypeStruct(flat, bf16),
            jax.ShapeDtypeStruct(flat, f32),
            jax.ShapeDtypeStruct(flat, bf16),
            jax.ShapeDtypeStruct(flat, bf16),
            jax.ShapeDtypeStruct((1, rows), bf16),
            jax.ShapeDtypeStruct((1, rows), bf16),
        ],
        in_specs=[smem, vmem, vmem],
        out_specs=[vmem] * 6,
        scratch_shapes=[stage, stage, stage],
        compiler_params=pltpu.CompilerParams(vmem_limit_bytes=24 * 1024 * 1024),
        name="adam",
    )(slots, arrived, to_tiles(gradient))
    blocks = [from_tiles(x, rows, cols) for x in outs[:4]]
    return (*blocks, outs[4].reshape(rows), outs[5].reshape(rows))


def routes(old_map, block_rows, peer_cap):
    self_index = lax.axis_index(ALL)
    my_slots = self_index * block_rows + jnp.arange(block_rows, dtype=jnp.int32)
    block_ids = jnp.arange(old_map.shape[0], dtype=jnp.int32)
    held = jnp.sum(jnp.where(old_map[None, :] == my_slots[:, None], block_ids[None, :], 0), axis=1)
    target = held // block_rows
    sent_rank = pair_rank(target, held % block_rows)
    wanted = lax.dynamic_slice_in_dim(old_map, self_index * block_rows, block_rows)
    source = wanted // block_rows
    got_rank = pair_rank(source, jnp.arange(block_rows, dtype=jnp.int32))
    return target * peer_cap + sent_rank, source * peer_cap + got_rank


def local(grad_parts, old_master, old_mean, old_mean_scale, old_square, old_square_scale, old_map):
    count_all = lax.axis_size(ALL)
    block_rows, block_len = old_master.shape
    peer_cap = 2
    slot_total = count_all * peer_cap
    chunks = block_len // LANES
    gradient = lax.psum_scatter(grad_parts[0], "dp", scatter_dimension=0, tiled=True)
    send_slot, recv_slot = routes(old_map, block_rows, peer_cap)
    packed = pack(
        send_slot,
        old_mean_scale.astype(jnp.float32),
        old_square_scale.astype(jnp.float32),
        old_master,
        old_mean,
        old_square,
        slot_total,
    )
    arrived = lax.all_to_all(
        packed.reshape(count_all, peer_cap * 3 * chunks, LANES), ALL, split_axis=0, concat_axis=0, tiled=True
    ).reshape(slot_total, 3 * chunks, LANES)
    mine, master, mean_codes, square_codes, mean_scales, square_scales = adam(recv_slot, arrived, gradient)
    weights = lax.all_gather(mine, "dp", axis=0, tiled=True)
    return (weights, master, mean_codes, mean_scales, square_codes, square_scales)


def solution(mesh):
    in_specs = (
        P("dp", "fsdp", None),
        P(ALL, None),
        P(ALL, None),
        P(ALL),
        P(ALL, None),
        P(ALL),
        P(),
    )
    out_specs = (
        P("fsdp", None),
        P(ALL, None),
        P(ALL, None),
        P(ALL),
        P(ALL, None),
        P(ALL),
    )
    return jax.shard_map(local, mesh=mesh, in_specs=in_specs, out_specs=out_specs, check_vma=False)
```

```python
import functools

import jax
import jax.numpy as jnp
from jax import lax
from jax.experimental import pallas as pl
from jax.experimental.pallas import tpu as pltpu
from jax.sharding import PartitionSpec as P

ALL = ("fsdp", "dp")
LANES = 128
SUB = 8
RING = 4
CORES = 2
STEPS = (2, 1, 3, 0)
FAR = ((2, 0), (2, 1), (1, 1), (3, 0))
NEAR = ((1, 0), (3, 1))


def to_tiles(values):
    rows, cols = values.shape
    tiled = values.reshape(rows // SUB, SUB, cols // LANES, LANES)
    return tiled.transpose(0, 2, 1, 3).reshape(rows * cols // LANES, LANES)


def from_tiles(values, rows, cols):
    tiled = values.reshape(rows // SUB, cols // LANES, SUB, LANES)
    return tiled.transpose(0, 2, 1, 3).reshape(rows, cols)


def pair_rank(owners, keyed):
    matching = owners[:, None] == owners[None, :]
    before = keyed[None, :] < keyed[:, None]
    return jnp.sum(jnp.where(matching & before, 1, 0), axis=1).astype(jnp.int32)


def pack_kernel(rows, chunks, slot_ref, mscale_ref, sscale_ref, master_ref, mean_ref, square_ref, out_ref, wide_mean, wide_square):
    wide_mean[...] = mean_ref[...].astype(jnp.float32)
    wide_square[...] = square_ref[...].astype(jnp.float32)
    for row in range(rows):
        base = (row // SUB) * chunks * SUB + row % SUB
        spots = pl.ds(base, chunks, stride=SUB)
        slot = slot_ref[row]
        out_ref[slot, pl.ds(0, chunks), :] = master_ref[spots, :].astype(jnp.bfloat16)
        out_ref[slot, pl.ds(chunks, chunks), :] = (wide_mean[spots, :] * mscale_ref[row]).astype(jnp.bfloat16)
        out_ref[slot, pl.ds(2 * chunks, chunks), :] = (wide_square[spots, :] * sscale_ref[row]).astype(jnp.bfloat16)


def pack(slots, mean_scale, square_scale, master, mean, square, slot_total):
    rows, cols = master.shape
    chunks = cols // LANES
    smem = pl.BlockSpec(memory_space=pltpu.SMEM)
    vmem = pl.BlockSpec(memory_space=pltpu.VMEM)
    flat = (rows * chunks, LANES)
    return pl.pallas_call(
        functools.partial(pack_kernel, rows, chunks),
        out_shape=jax.ShapeDtypeStruct((slot_total, 3 * chunks, LANES), jnp.bfloat16),
        in_specs=[smem, smem, smem, vmem, vmem, vmem],
        out_specs=vmem,
        scratch_shapes=[pltpu.VMEM(flat, jnp.float32), pltpu.VMEM(flat, jnp.float32)],
        compiler_params=pltpu.CompilerParams(vmem_limit_bytes=24 * 1024 * 1024),
        name="pack",
    )(slots, mean_scale, square_scale, to_tiles(master), to_tiles(mean), to_tiles(square))


def adam_kernel(rows, chunks, slot_ref, in_ref, own_ref, sib_ref, up_lo_ref, up_hi_ref, dn_lo_ref, dn_hi_ref, weights_ref, master_ref, mcode_ref, scode_ref, mscale_ref, sscale_ref, weight_old, mean_old, square_old):
    span = chunks * SUB
    lane = lax.broadcasted_iota(jnp.int32, (SUB, LANES), 1)
    sub = lax.broadcasted_iota(jnp.int32, (SUB, LANES), 0)
    mline = jnp.zeros((SUB, LANES), jnp.float32)
    sline = jnp.zeros((SUB, LANES), jnp.float32)
    for group in range(rows // SUB):
        buf = group % 2
        for r in range(SUB):
            slot = slot_ref[group * SUB + r]
            spots = pl.ds(buf * span + r, chunks, stride=SUB)
            weight_old[spots, :] = in_ref[slot, pl.ds(0, chunks), :].astype(jnp.float32)
            mean_old[spots, :] = in_ref[slot, pl.ds(chunks, chunks), :].astype(jnp.float32)
            square_old[spots, :] = in_ref[slot, pl.ds(2 * chunks, chunks), :].astype(jnp.float32)
        here = pl.ds(buf * span, span)
        there = pl.ds(group * span, span)
        low = group < rows // SUB // 2
        part = there if low else pl.ds((group - rows // SUB // 2) * span, span)
        up_ref, dn_ref = (up_lo_ref, dn_lo_ref) if low else (up_hi_ref, dn_hi_ref)
        gradient = own_ref[there, :].astype(jnp.float32) + sib_ref[there, :].astype(jnp.float32)
        gradient += up_ref[part, :].astype(jnp.float32) + dn_ref[part, :].astype(jnp.float32)
        old = weight_old[here, :]
        mean_next = 0.9 * mean_old[here, :] + 0.1 * gradient
        square_next = 0.95 * square_old[here, :] + 0.05 * gradient * gradient
        master = old - 0.05 * (mean_next / (jnp.sqrt(square_next) + 1e-08) + 0.1 * old)
        master_ref[there, :] = master
        weights_ref[there, :] = master.astype(jnp.bfloat16)
        mean_next = mean_next.reshape(chunks, SUB, LANES)
        square_next = square_next.reshape(chunks, SUB, LANES)
        mpeak = jnp.max(jnp.max(jnp.abs(mean_next), axis=0), axis=1, keepdims=True)
        speak = jnp.max(jnp.max(square_next, axis=0), axis=1, keepdims=True)
        mscale = (mpeak + 1e-06).astype(jnp.bfloat16).astype(jnp.float32)
        sscale = (speak + 1e-06).astype(jnp.bfloat16).astype(jnp.float32)
        mcode_ref[there, :] = (mean_next * (1.0 / mscale)[None]).reshape(span, LANES).astype(jnp.bfloat16)
        scode_ref[there, :] = (square_next * (1.0 / sscale)[None]).reshape(span, LANES).astype(jnp.bfloat16)
        mine = lane == sub + group * SUB
        mline = jnp.where(mine, mscale, mline)
        sline = jnp.where(mine, sscale, sline)
    mscale_ref[...] = jnp.sum(mline, axis=0, keepdims=True).astype(jnp.bfloat16)
    sscale_ref[...] = jnp.sum(sline, axis=0, keepdims=True).astype(jnp.bfloat16)


def adam(slots, arrived, grads, rows, chunks):
    flat = (rows * chunks, LANES)
    bf16, f32 = jnp.bfloat16, jnp.float32
    stage = pltpu.VMEM((2 * chunks * SUB, LANES), f32)
    vmem = pl.BlockSpec(memory_space=pltpu.VMEM)
    outs = pl.pallas_call(
        functools.partial(adam_kernel, rows, chunks),
        out_shape=[
            jax.ShapeDtypeStruct(flat, bf16),
            jax.ShapeDtypeStruct(flat, f32),
            jax.ShapeDtypeStruct(flat, bf16),
            jax.ShapeDtypeStruct(flat, bf16),
            jax.ShapeDtypeStruct((1, rows), bf16),
            jax.ShapeDtypeStruct((1, rows), bf16),
        ],
        in_specs=[pl.BlockSpec(memory_space=pltpu.SMEM)] + [vmem] * 7,
        out_specs=[vmem] * 6,
        scratch_shapes=[stage, stage, stage],
        compiler_params=pltpu.CompilerParams(vmem_limit_bytes=24 * 1024 * 1024),
        name="adam",
    )(slots, arrived, *grads)
    return outs


def place():
    me = lax.axis_index("dp")
    return me // CORES, me % CORES


def shard_at(y, step, core):
    return lax.rem(y + step, RING) * CORES + core


def sends(shift, flip):
    return [
        (y * CORES + c, (y + shift) % RING * CORES + (CORES - 1 - c if flip else c))
        for y in range(RING)
        for c in range(CORES)
    ]


def send(values, shift, flip=False):
    return lax.ppermute(values, "dp", sends(shift, flip))


def cut_kernel(grad_ref, far_ref, near_ref, sems):
    y, core = place()
    copies = []
    for k, step in enumerate(STEPS):
        target = far_ref.at[k] if k < 3 else near_ref
        copies.append(pltpu.make_async_copy(grad_ref.at[shard_at(y, step, CORES - 1 - core)], target, sems.at[k]))
    for copy in copies:
        copy.start()
    for copy in copies:
        copy.wait()


def cut(grads):
    _, span, lanes = grads.shape
    hbm = pl.BlockSpec(memory_space=pltpu.HBM)
    return pl.pallas_call(
        cut_kernel,
        out_shape=[
            jax.ShapeDtypeStruct((3, span, lanes), grads.dtype),
            jax.ShapeDtypeStruct((span, lanes), grads.dtype),
        ],
        in_specs=[hbm],
        out_specs=[hbm, hbm],
        scratch_shapes=[pltpu.SemaphoreType.DMA((4,))],
        name="cut",
    )(grads)


def keep_kernel(half, grad_ref, far_ref, near_ref, own_ref, sems):
    y, core = place()
    jobs = [(step, part * half, half, far_ref.at[k]) for k, (step, part) in enumerate(FAR)]
    jobs += [(step, part * half, half, near_ref.at[k]) for k, (step, part) in enumerate(NEAR)]
    jobs += [(0, 0, 2 * half, own_ref)]
    copies = [
        pltpu.make_async_copy(grad_ref.at[shard_at(y, step, core), pl.ds(start, size)], target, sems.at[k])
        for k, (step, start, size, target) in enumerate(jobs)
    ]
    for copy in copies:
        copy.start()
    for copy in copies:
        copy.wait()


def keep(grads):
    _, span, lanes = grads.shape
    half = span // 2
    hbm = pl.BlockSpec(memory_space=pltpu.HBM)
    shapes = [(len(FAR), half, lanes), (len(NEAR), half, lanes), (span, lanes)]
    return pl.pallas_call(
        functools.partial(keep_kernel, half),
        out_shape=[jax.ShapeDtypeStruct(shape, grads.dtype) for shape in shapes],
        in_specs=[hbm],
        out_specs=[hbm] * 3,
        scratch_shapes=[pltpu.SemaphoreType.DMA((len(FAR) + len(NEAR) + 1,))],
        name="keep",
    )(grads)


def add_kernel(half, jobs, own_ref, got_ref, *refs):
    more_refs, out_refs = refs[: -len(jobs)], refs[-len(jobs) :]
    for k, (step, part) in enumerate(jobs):
        total = own_ref[k].astype(jnp.float32)
        total += got_ref[STEPS.index(step), pl.ds(part * half, half), :].astype(jnp.float32)
        if more_refs:
            total += more_refs[k][...].astype(jnp.float32)
        out_refs[k][...] = total.astype(own_ref.dtype)


def add(jobs, own, got, *more):
    _, half, lanes = own.shape
    vmem = pl.BlockSpec(memory_space=pltpu.VMEM)
    return pl.pallas_call(
        functools.partial(add_kernel, half, jobs),
        out_shape=[jax.ShapeDtypeStruct((half, lanes), own.dtype)] * len(jobs),
        in_specs=[vmem] * (2 + len(more)),
        out_specs=[vmem] * len(jobs),
        compiler_params=pltpu.CompilerParams(vmem_limit_bytes=16 * 1024 * 1024),
        name="add_near" if more else "add_far",
    )(own, got, *more)


def reduce_shards(grads, far, near):
    far_got = send(far, 0, True)
    near_got = send(near, 0, True)
    own_far, own_near, own = keep(grads)
    opp_lo, opp_hi, up_hi, dn_lo = add(FAR, own_far, far_got)
    up_got = send(opp_lo, 1)
    dn_got = send(opp_hi, 3)
    up_hi_got = send(up_hi, 1)
    dn_lo_got = send(dn_lo, 3)
    up_lo, dn_hi = add(NEAR, own_near, far_got, up_got, dn_got)
    up_lo_got = send(up_lo, 1)
    dn_hi_got = send(dn_hi, 3)
    return own, near_got, up_lo_got, up_hi_got, dn_lo_got, dn_hi_got


def join_kernel(span, starts, *refs):
    parts, (out_ref, sems) = refs[: len(starts)], refs[-2:]
    y, core = place()
    copies = []
    for k, (step, flip, offset) in enumerate(starts):
        side = CORES - 1 - core if flip else core
        base = pl.multiple_of(shard_at(y, step, side) * span + offset, span // 2)
        copies.append(pltpu.make_async_copy(parts[k], out_ref.at[pl.ds(base, parts[k].shape[0])], sems.at[k]))
    for copy in copies:
        copy.start()
    for copy in copies:
        copy.wait()


def join(span, starts, parts, whole=None):
    lanes = parts[0].shape[1]
    hbm = pl.BlockSpec(memory_space=pl.ANY)
    given = list(parts) + ([] if whole is None else [whole])
    return pl.pallas_call(
        functools.partial(join_kernel, span, starts),
        out_shape=jax.ShapeDtypeStruct((RING * CORES * span, lanes), parts[0].dtype),
        in_specs=[hbm] * len(given),
        out_specs=hbm,
        scratch_shapes=[pltpu.SemaphoreType.DMA((len(parts),))],
        input_output_aliases={} if whole is None else {len(parts): 0},
        name="join",
    )(*given)


def gather_shards(mine):
    span = mine.shape[0]
    half = span // 2
    up, dn, sib = send(mine, 1), send(mine, 3), send(mine, 0, True)
    opp_lo, opp_hi = send(up[:half], 1), send(dn[half:], 3)
    up_sib, dn_sib = send(up, 0, True), send(dn, 0, True)
    starts = [(0, 0, 0), (0, 1, 0), (3, 0, 0), (1, 0, 0), (3, 1, 0), (1, 1, 0)]
    most = join(span, starts, [mine, sib, up, dn, up_sib, dn_sib])
    starts = [(2, 0, 0), (2, 0, half), (2, 1, 0), (2, 1, half)]
    return join(span, starts, [opp_lo, opp_hi, send(opp_lo, 0, True), send(opp_hi, 0, True)], most)


def routes(old_map, block_rows, peer_cap):
    self_index = lax.axis_index(ALL)
    my_slots = self_index * block_rows + jnp.arange(block_rows, dtype=jnp.int32)
    block_ids = jnp.arange(old_map.shape[0], dtype=jnp.int32)
    held = jnp.sum(jnp.where(old_map[None, :] == my_slots[:, None], block_ids[None, :], 0), axis=1)
    target = held // block_rows
    sent_rank = pair_rank(target, held % block_rows)
    wanted = lax.dynamic_slice_in_dim(old_map, self_index * block_rows, block_rows)
    source = wanted // block_rows
    got_rank = pair_rank(source, jnp.arange(block_rows, dtype=jnp.int32))
    return target * peer_cap + sent_rank, source * peer_cap + got_rank


def local(grad_parts, old_master, old_mean, old_mean_scale, old_square, old_square_scale, old_map):
    count_all = lax.axis_size(ALL)
    block_rows, block_len = old_master.shape
    peer_cap = 2
    slot_total = count_all * peer_cap
    chunks = block_len // LANES
    grads = to_tiles(grad_parts[0]).reshape(RING * CORES, block_rows * chunks, LANES)
    far, near, old_map = lax.optimization_barrier((*cut(grads), old_map))
    addends = reduce_shards(grads, far, near)
    send_slot, recv_slot = routes(old_map, block_rows, peer_cap)
    packed = pack(
        send_slot,
        old_mean_scale.astype(jnp.float32),
        old_square_scale.astype(jnp.float32),
        old_master,
        old_mean,
        old_square,
        slot_total,
    )
    arrived = lax.all_to_all(
        packed.reshape(count_all, peer_cap * 3 * chunks, LANES), ALL, split_axis=0, concat_axis=0, tiled=True
    ).reshape(slot_total, 3 * chunks, LANES)
    mine, *blocks, mean_scales, square_scales = adam(recv_slot, arrived, addends, block_rows, chunks)
    master, mean_codes, square_codes = (from_tiles(x, block_rows, block_len) for x in blocks)
    weights = from_tiles(gather_shards(mine), RING * CORES * block_rows, block_len)
    return (weights, master, mean_codes, mean_scales.reshape(-1), square_codes, square_scales.reshape(-1))


def solution(mesh):
    in_specs = (
        P("dp", "fsdp", None),
        P(ALL, None),
        P(ALL, None),
        P(ALL),
        P(ALL, None),
        P(ALL),
        P(),
    )
    out_specs = (
        P("fsdp", None),
        P(ALL, None),
        P(ALL, None),
        P(ALL),
        P(ALL, None),
        P(ALL),
    )
    return jax.shard_map(local, mesh=mesh, in_specs=in_specs, out_specs=out_specs, check_vma=False)
```

```python
import functools

import jax
import jax.numpy as jnp
from jax import lax
from jax.experimental import pallas as pl
from jax.experimental.pallas import tpu as pltpu
from jax.sharding import PartitionSpec as P

ALL = ("fsdp", "dp")
LANES = 128
SUB = 8
RING = 4
CORES = 2
ADDENDS = 3


def to_tiles(values):
    rows, cols = values.shape
    tiled = values.reshape(rows // SUB, SUB, cols // LANES, LANES)
    return tiled.transpose(0, 2, 1, 3).reshape(rows * cols // LANES, LANES)


def from_tiles(values, rows, cols):
    tiled = values.reshape(rows // SUB, cols // LANES, SUB, LANES)
    return tiled.transpose(0, 2, 1, 3).reshape(rows, cols)


def pair_rank(owners, keyed):
    matching = owners[:, None] == owners[None, :]
    before = keyed[None, :] < keyed[:, None]
    return jnp.sum(jnp.where(matching & before, 1, 0), axis=1).astype(jnp.int32)


def send_slots(block_map, rows):
    owners = block_map.shape[0]
    first_slot = (lax.axis_index("fsdp") * lax.axis_size("dp") + lax.axis_index("dp")) * rows
    held = block_map - first_slot
    here = (held >= 0) & (held < rows)
    spot = lax.broadcasted_iota(jnp.int32, block_map.shape, 1)
    first = jnp.min(jnp.where(here, spot, rows), axis=1, keepdims=True)
    one = jnp.max(jnp.where(here & (spot == first), held, -1), axis=1, keepdims=True)
    two = jnp.max(jnp.where(here & (spot > first), held, -1), axis=1, keepdims=True)
    owner = lax.broadcasted_iota(jnp.int32, (owners, rows), 0)
    slot = lax.broadcasted_iota(jnp.int32, (owners, rows), 1)
    place_of = jnp.where(one == slot, 2 * owner, 0) + jnp.where(two == slot, 2 * owner + 1, 0)
    return jnp.sum(place_of, axis=0, keepdims=True)


def pack_kernel(rows, chunks, map_ref, mscale_ref, sscale_ref, master_ref, mean_ref, square_ref, out_ref, *scratch):
    held_map, master, mean, square, wide_mean, wide_square, slots, mscale, sscale, slot_of, mscale_of, sscale_of = scratch[:12]
    load_sems, table_sems = scratch[12:]
    pairs = [(map_ref, held_map), (mean_ref, mean), (square_ref, square), (master_ref, master)]
    loads = [pltpu.make_async_copy(ref, room, load_sems.at[k]) for k, (ref, room) in enumerate(pairs)]
    for load in loads:
        load.start()
    mscale[...] = mscale_ref[...].astype(jnp.float32)
    sscale[...] = sscale_ref[...].astype(jnp.float32)
    loads[0].wait()
    slots[...] = send_slots(held_map[...], rows)
    tables = [(slots, slot_of), (mscale, mscale_of), (sscale, sscale_of)]
    tables = [pltpu.make_async_copy(table, room, table_sems.at[k]) for k, (table, room) in enumerate(tables)]
    for table in tables:
        table.start()
    loads[1].wait()
    wide_mean[...] = mean[...].astype(jnp.float32)
    loads[2].wait()
    wide_square[...] = square[...].astype(jnp.float32)
    for table in tables:
        table.wait()
    loads[3].wait()
    for row in range(rows):
        base = (row // SUB) * chunks * SUB + row % SUB
        spots = pl.ds(base, chunks, stride=SUB)
        slot = slot_of[0, row]
        out_ref[slot, pl.ds(0, chunks), :] = master[spots, :].astype(jnp.bfloat16)
        out_ref[slot, pl.ds(chunks, chunks), :] = (wide_mean[spots, :] * mscale_of[0, row]).astype(jnp.bfloat16)
        out_ref[slot, pl.ds(2 * chunks, chunks), :] = (wide_square[spots, :] * sscale_of[0, row]).astype(jnp.bfloat16)


def pack(old_map, mean_scale, square_scale, master, mean, square, slot_total):
    rows, cols = master.shape
    chunks = cols // LANES
    hbm = pl.BlockSpec(memory_space=pl.ANY)
    vmem = pl.BlockSpec(memory_space=pltpu.VMEM)
    flat = (rows * chunks, LANES)
    f32, i32 = jnp.float32, jnp.int32
    block_map = old_map.reshape(-1, rows)
    return pl.pallas_call(
        functools.partial(pack_kernel, rows, chunks),
        out_shape=jax.ShapeDtypeStruct((slot_total, 3 * chunks, LANES), jnp.bfloat16),
        in_specs=[hbm, vmem, vmem, hbm, hbm, hbm],
        out_specs=vmem,
        scratch_shapes=[
            pltpu.VMEM(block_map.shape, i32),
            pltpu.VMEM(flat, f32),
            pltpu.VMEM(flat, mean.dtype),
            pltpu.VMEM(flat, square.dtype),
            pltpu.VMEM(flat, f32),
            pltpu.VMEM(flat, f32),
            pltpu.VMEM((1, rows), i32),
            pltpu.VMEM((1, rows), f32),
            pltpu.VMEM((1, rows), f32),
            pltpu.SMEM((1, rows), i32),
            pltpu.SMEM((1, rows), f32),
            pltpu.SMEM((1, rows), f32),
            pltpu.SemaphoreType.DMA((4,)),
            pltpu.SemaphoreType.DMA((3,)),
        ],
        compiler_params=pltpu.CompilerParams(vmem_limit_bytes=56 * 1024 * 1024),
        name="pack",
    )(
        block_map,
        mean_scale.reshape(1, rows),
        square_scale.reshape(1, rows),
        to_tiles(master),
        to_tiles(mean),
        to_tiles(square),
    )


def unpack_kernel(rows, chunks, slot_ref, in_ref, out_ref, weight_old, mean_old, square_old):
    span = chunks * SUB
    stages = (weight_old, mean_old, square_old)
    for group in range(rows // SUB):
        buf = group % 2
        for r in range(SUB):
            slot = slot_ref[group * SUB + r]
            spots = pl.ds(buf * span + r, chunks, stride=SUB)
            for k, stage in enumerate(stages):
                stage[spots, :] = in_ref[slot, pl.ds(k * chunks, chunks), :].astype(jnp.float32)
        for k, stage in enumerate(stages):
            out_ref[k, pl.ds(group * span, span), :] = stage[pl.ds(buf * span, span), :].astype(out_ref.dtype)


def unpack(slots, arrived, rows, chunks):
    stage = pltpu.VMEM((2 * chunks * SUB, LANES), jnp.float32)
    vmem = pl.BlockSpec(memory_space=pltpu.VMEM)
    return pl.pallas_call(
        functools.partial(unpack_kernel, rows, chunks),
        out_shape=jax.ShapeDtypeStruct((3, rows * chunks, LANES), arrived.dtype),
        in_specs=[pl.BlockSpec(memory_space=pltpu.SMEM), vmem],
        out_specs=vmem,
        scratch_shapes=[stage, stage, stage],
        compiler_params=pltpu.CompilerParams(vmem_limit_bytes=24 * 1024 * 1024),
        name="unpack",
    )(slots, arrived)


def adam_kernel(rows, chunks, old_ref, mine_ref, *refs):
    side_refs, refs = refs[:4], refs[4:]
    weights_ref, master_ref, mcode_ref, scode_ref, mscale_ref, sscale_ref = refs[:6]
    old, addends, sems = refs[6:]
    span = chunks * SUB
    groups = rows // SUB
    half = groups // 2 * span
    loads = []
    for h in range(2):
        part = pl.ds(h * half, half)
        pairs = [(mine_ref.at[part], addends.at[0, part])]
        pairs += [(side_refs[2 * k + h], addends.at[1 + k, part]) for k in range(2)]
        pairs += [(old_ref.at[k, part], old.at[k, part]) for k in range(3)]
        loads.append([pltpu.make_async_copy(ref, room, sems.at[h, k]) for k, (ref, room) in enumerate(pairs)])
    for load in loads[0] + loads[1]:
        load.start()
    lane = lax.broadcasted_iota(jnp.int32, (SUB, LANES), 1)
    sub = lax.broadcasted_iota(jnp.int32, (SUB, LANES), 0)
    mline = jnp.zeros((SUB, LANES), jnp.float32)
    sline = jnp.zeros((SUB, LANES), jnp.float32)
    for group in range(groups):
        if group % (groups // 2) == 0:
            for load in loads[group * 2 // groups]:
                load.wait()
        there = pl.ds(group * span, span)
        gradient = addends[0, there, :].astype(jnp.float32)
        for k in range(1, ADDENDS):
            gradient += addends[k, there, :].astype(jnp.float32)
        weight_old, mean_old, square_old = (old[k, there, :].astype(jnp.float32) for k in range(3))
        mean_next = 0.9 * mean_old + 0.1 * gradient
        square_next = 0.95 * square_old + 0.05 * gradient * gradient
        master = weight_old - 0.05 * (mean_next / (jnp.sqrt(square_next) + 1e-08) + 0.1 * weight_old)
        master_ref[there, :] = master
        weights_ref[there, :] = master.astype(jnp.bfloat16)
        mean_next = mean_next.reshape(chunks, SUB, LANES)
        square_next = square_next.reshape(chunks, SUB, LANES)
        mpeak = jnp.max(jnp.max(jnp.abs(mean_next), axis=0), axis=1, keepdims=True)
        speak = jnp.max(jnp.max(square_next, axis=0), axis=1, keepdims=True)
        mscale = (mpeak + 1e-06).astype(jnp.bfloat16).astype(jnp.float32)
        sscale = (speak + 1e-06).astype(jnp.bfloat16).astype(jnp.float32)
        mcode_ref[there, :] = (mean_next * (1.0 / mscale)[None]).reshape(span, LANES).astype(jnp.bfloat16)
        scode_ref[there, :] = (square_next * (1.0 / sscale)[None]).reshape(span, LANES).astype(jnp.bfloat16)
        mine = lane == sub + group * SUB
        mline = jnp.where(mine, mscale, mline)
        sline = jnp.where(mine, sscale, sline)
    mscale_ref[...] = jnp.sum(mline, axis=0, keepdims=True).astype(jnp.bfloat16)
    sscale_ref[...] = jnp.sum(sline, axis=0, keepdims=True).astype(jnp.bfloat16)


def adam(old, addends, rows, chunks):
    flat = (rows * chunks, LANES)
    bf16, f32 = jnp.bfloat16, jnp.float32
    vmem = pl.BlockSpec(memory_space=pltpu.VMEM)
    return pl.pallas_call(
        functools.partial(adam_kernel, rows, chunks),
        out_shape=[
            jax.ShapeDtypeStruct(flat, bf16),
            jax.ShapeDtypeStruct(flat, f32),
            jax.ShapeDtypeStruct(flat, bf16),
            jax.ShapeDtypeStruct(flat, bf16),
            jax.ShapeDtypeStruct((1, rows), bf16),
            jax.ShapeDtypeStruct((1, rows), bf16),
        ],
        in_specs=[pl.BlockSpec(memory_space=pl.ANY)] * 6,
        out_specs=[vmem] * 6,
        scratch_shapes=[
            pltpu.VMEM((3, *flat), bf16),
            pltpu.VMEM((ADDENDS, *flat), bf16),
            pltpu.SemaphoreType.DMA((2, 3 + ADDENDS)),
        ],
        compiler_params=pltpu.CompilerParams(vmem_limit_bytes=56 * 1024 * 1024),
        name="adam",
    )(old, *addends)


def place():
    me = lax.axis_index("dp")
    return me // CORES, me % CORES


def shard_at(y, step, core):
    return lax.rem(y + step, RING) * CORES + core


def sends(shift, flip):
    return [
        (y * CORES + c, (y + shift) % RING * CORES + (CORES - 1 - c if flip else c))
        for y in range(RING)
        for c in range(CORES)
    ]


def send(values, shift, flip=False):
    return lax.ppermute(values, "dp", sends(shift, flip))


def cut_kernel(shards, grad_ref, *refs):
    out_refs, (room, in_sems, out_sems) = refs[: len(shards)], refs[len(shards) :]
    y, core = place()
    loads, stores = [], []
    for k, (step, flip) in enumerate(shards):
        shard = shard_at(y, step, CORES - 1 - core if flip else core)
        loads.append(pltpu.make_async_copy(grad_ref.at[shard], room.at[k], in_sems.at[k]))
        stores.append(pltpu.make_async_copy(room.at[k], out_refs[k], out_sems.at[k]))
    for load in loads:
        load.start()
    for load, store in zip(loads, stores):
        load.wait()
        store.start()
    for store in stores:
        store.wait()


def cut(grads, shards):
    _, span, lanes = grads.shape
    count = len(shards)
    hbm = pl.BlockSpec(memory_space=pl.ANY)
    return pl.pallas_call(
        functools.partial(cut_kernel, shards),
        out_shape=[jax.ShapeDtypeStruct((span, lanes), grads.dtype)] * count,
        in_specs=[hbm],
        out_specs=[hbm] * count,
        scratch_shapes=[pltpu.VMEM((count, span, lanes), grads.dtype)] + [pltpu.SemaphoreType.DMA((count,))] * 2,
        compiler_params=pltpu.CompilerParams(vmem_limit_bytes=56 * 1024 * 1024),
        name="cut",
    )(grads)


def add_kernel(windows, sums, *refs):
    count, outs = len(windows), len(sums)
    in_refs, out_refs, rooms, totals = refs[:count], refs[count:][:outs], refs[count + outs :][:count], refs[2 * count + outs : -2]
    in_sems, out_sems = refs[-2:]
    loads = [
        pltpu.make_async_copy(ref.at[pl.ds(*window)], room, in_sems.at[k])
        for k, (ref, window, room) in enumerate(zip(in_refs, windows, rooms))
    ]
    for load in loads:
        load.start()
    stores = []
    for k, terms in enumerate(sums):
        total = None
        for term in terms:
            loads[term].wait()
            values = rooms[term][...].astype(jnp.float32)
            total = values if total is None else total + values
        totals[k][...] = total.astype(totals[k].dtype)
        store = pltpu.make_async_copy(totals[k], out_refs[k], out_sems.at[k])
        store.start()
        stores.append(store)
    for store in stores:
        store.wait()


def add(*sums):
    terms = [term for parts in sums for term in parts]
    lanes, dtype = terms[0][0].shape[1], terms[0][0].dtype
    hbm = pl.BlockSpec(memory_space=pl.ANY)
    order, at = [], 0
    for parts in sums:
        order.append(tuple(range(at, at + len(parts))))
        at += len(parts)
    windows = [(first, rows) for _, first, rows in terms]
    shapes = [(rows, lanes) for _, rows in windows]
    outs = [(parts[0][2], lanes) for parts in sums]
    return pl.pallas_call(
        functools.partial(add_kernel, windows, order),
        out_shape=[jax.ShapeDtypeStruct(shape, dtype) for shape in outs],
        in_specs=[hbm] * len(terms),
        out_specs=[hbm] * len(outs),
        scratch_shapes=[pltpu.VMEM(shape, dtype) for shape in shapes + outs]
        + [pltpu.SemaphoreType.DMA((len(terms),)), pltpu.SemaphoreType.DMA((len(outs),))],
        compiler_params=pltpu.CompilerParams(vmem_limit_bytes=56 * 1024 * 1024),
        name="add",
    )(*[array for array, _, _ in terms])


def reduce_shards(grads, arrived):
    span = grads.shape[1]
    half = span // 2
    steps = (2, 1, 3, 0)
    got = dict(zip(steps, [send(part, 0, True) for part in cut(grads, tuple((step, 1) for step in steps))]))
    own = dict(zip(steps, cut(grads, tuple((step, 0) for step in steps))))

    def both(step, first, rows):
        return [(own[step], first, rows), (got[step], first, rows)]

    opp_lo, opp_hi, up_hi, dn_lo, mine = add(
        both(2, 0, half), both(2, half, half), both(1, half, half), both(3, 0, half), both(0, 0, span)
    )
    opp_up, opp_dn = send(opp_lo, 1), send(opp_hi, 3)
    up_hi_got, dn_lo_got = send(up_hi, 1), send(dn_lo, 3)
    opp_up, opp_dn, arrived = lax.optimization_barrier((opp_up, opp_dn, arrived))
    up_lo, dn_hi = add(both(1, 0, half) + [(opp_up, 0, half)], both(3, half, half) + [(opp_dn, 0, half)])
    return (mine, send(up_lo, 1), up_hi_got, dn_lo_got, send(dn_hi, 3)), arrived


def join_kernel(span, starts, *refs):
    parts, (out_ref, *rooms, in_sems, sems) = refs[: len(starts)], refs[-3 - len(starts) :]
    y, core = place()
    loads = [pltpu.make_async_copy(part, room, in_sems.at[k]) for k, (part, room) in enumerate(zip(parts, rooms))]
    for load in loads:
        load.start()
    copies = []
    for k, (step, flip, offset) in enumerate(starts):
        side = CORES - 1 - core if flip else core
        base = pl.multiple_of(shard_at(y, step, side) * span + offset, span // 2)
        copies.append(pltpu.make_async_copy(rooms[k], out_ref.at[pl.ds(base, parts[k].shape[0])], sems.at[k]))
    for load, copy in zip(loads, copies):
        load.wait()
        copy.start()
    for copy in copies:
        copy.wait()


def join(span, starts, parts, whole=None):
    lanes = parts[0].shape[1]
    hbm = pl.BlockSpec(memory_space=pl.ANY)
    given = list(parts) + ([] if whole is None else [whole])
    return pl.pallas_call(
        functools.partial(join_kernel, span, starts),
        out_shape=jax.ShapeDtypeStruct((RING * CORES * span, lanes), parts[0].dtype),
        in_specs=[hbm] * len(given),
        out_specs=hbm,
        scratch_shapes=[pltpu.VMEM(part.shape, part.dtype) for part in parts]
        + [pltpu.SemaphoreType.DMA((len(parts),))] * 2,
        compiler_params=pltpu.CompilerParams(vmem_limit_bytes=16 * 1024 * 1024),
        input_output_aliases={} if whole is None else {len(parts): 0},
        name="join",
    )(*given)


def gather_shards(mine):
    span = mine.shape[0]
    half = span // 2
    up, dn, sib = send(mine, 1), send(mine, 3), send(mine, 0, True)
    opp_lo, opp_hi = send(up[:half], 1), send(dn[half:], 3)
    up_sib, dn_sib = send(up, 0, True), send(dn, 0, True)
    starts = [(0, 0, 0), (0, 1, 0), (3, 0, 0), (1, 0, 0), (3, 1, 0), (1, 1, 0)]
    most = join(span, starts, [mine, sib, up, dn, up_sib, dn_sib])
    most, opp_lo, opp_hi = lax.optimization_barrier((most, opp_lo, opp_hi))
    starts = [(2, 0, 0), (2, 0, half), (2, 1, 0), (2, 1, half)]
    return join(span, starts, [opp_lo, opp_hi, send(opp_lo, 0, True), send(opp_hi, 0, True)], most)


def arrivals(old_map, block_rows, peer_cap):
    self_index = lax.axis_index(ALL)
    wanted = lax.dynamic_slice_in_dim(old_map, self_index * block_rows, block_rows)
    source = wanted // block_rows
    return source * peer_cap + pair_rank(source, jnp.arange(block_rows, dtype=jnp.int32))


def local(grad_parts, old_master, old_mean, old_mean_scale, old_square, old_square_scale, old_map):
    count_all = lax.axis_size(ALL)
    block_rows, block_len = old_master.shape
    peer_cap = 2
    slot_total = count_all * peer_cap
    chunks = block_len // LANES
    grads = to_tiles(grad_parts[0]).reshape(RING * CORES, block_rows * chunks, LANES)
    packed = pack(old_map, old_mean_scale, old_square_scale, old_master, old_mean, old_square, slot_total)
    packed, late_grads, late_map = lax.optimization_barrier((packed, grads, old_map))
    arrived = lax.all_to_all(
        packed.reshape(count_all, peer_cap * 3 * chunks, LANES), ALL, split_axis=0, concat_axis=0, tiled=True
    ).reshape(slot_total, 3 * chunks, LANES)
    addends, arrived = reduce_shards(late_grads, arrived)
    old = unpack(arrivals(late_map, block_rows, peer_cap), arrived, block_rows, chunks)
    mine, *blocks, mean_scales, square_scales = adam(old, addends, block_rows, chunks)
    master, mean_codes, square_codes = (from_tiles(x, block_rows, block_len) for x in blocks)
    weights = from_tiles(gather_shards(mine), RING * CORES * block_rows, block_len)
    return (weights, master, mean_codes, mean_scales.reshape(-1), square_codes, square_scales.reshape(-1))


def solution(mesh):
    in_specs = (
        P("dp", "fsdp", None),
        P(ALL, None),
        P(ALL, None),
        P(ALL),
        P(ALL, None),
        P(ALL),
        P(),
    )
    out_specs = (
        P("fsdp", None),
        P(ALL, None),
        P(ALL, None),
        P(ALL),
        P(ALL, None),
        P(ALL),
    )
    return jax.shard_map(local, mesh=mesh, in_specs=in_specs, out_specs=out_specs, check_vma=False)
```

```python
import functools

import jax
import jax.numpy as jnp
from jax import lax
from jax.experimental import pallas as pl
from jax.experimental.pallas import tpu as pltpu
from jax.sharding import PartitionSpec as P

ALL = ("fsdp", "dp")
LANES = 128
SUB = 8
RING = 4
CORES = 2
ADDENDS = 3


def to_tiles(values):
    rows, cols = values.shape
    tiled = values.reshape(rows // SUB, SUB, cols // LANES, LANES)
    return tiled.transpose(0, 2, 1, 3).reshape(rows * cols // LANES, LANES)


def from_tiles(values, rows, cols):
    tiled = values.reshape(rows // SUB, cols // LANES, SUB, LANES)
    return tiled.transpose(0, 2, 1, 3).reshape(rows, cols)


def pair_rank(owners, keyed):
    matching = owners[:, None] == owners[None, :]
    before = keyed[None, :] < keyed[:, None]
    return jnp.sum(jnp.where(matching & before, 1, 0), axis=1).astype(jnp.int32)


def send_slots(block_map, rows):
    owners = block_map.shape[0]
    first_slot = (lax.axis_index("fsdp") * lax.axis_size("dp") + lax.axis_index("dp")) * rows
    held = block_map - first_slot
    here = (held >= 0) & (held < rows)
    spot = lax.broadcasted_iota(jnp.int32, block_map.shape, 1)
    first = jnp.min(jnp.where(here, spot, rows), axis=1, keepdims=True)
    one = jnp.max(jnp.where(here & (spot == first), held, -1), axis=1, keepdims=True)
    two = jnp.max(jnp.where(here & (spot > first), held, -1), axis=1, keepdims=True)
    owner = lax.broadcasted_iota(jnp.int32, (owners, rows), 0)
    slot = lax.broadcasted_iota(jnp.int32, (owners, rows), 1)
    place_of = jnp.where(one == slot, 2 * owner, 0) + jnp.where(two == slot, 2 * owner + 1, 0)
    return jnp.sum(place_of, axis=0, keepdims=True)


def pack_kernel(rows, chunks, map_ref, mscale_ref, sscale_ref, master_ref, mean_ref, square_ref, out_ref, *scratch):
    held_map, master, mean, square, wide_mean, wide_square, slots, mscale, sscale, slot_of, mscale_of, sscale_of = scratch[:12]
    load_sems, table_sems = scratch[12:]
    pairs = [(map_ref, held_map), (mean_ref, mean), (square_ref, square), (master_ref, master)]
    loads = [pltpu.make_async_copy(ref, room, load_sems.at[k]) for k, (ref, room) in enumerate(pairs)]
    for load in loads:
        load.start()
    mscale[...] = mscale_ref[...].astype(jnp.float32)
    sscale[...] = sscale_ref[...].astype(jnp.float32)
    loads[0].wait()
    slots[...] = send_slots(held_map[...], rows)
    tables = [(slots, slot_of), (mscale, mscale_of), (sscale, sscale_of)]
    tables = [pltpu.make_async_copy(table, room, table_sems.at[k]) for k, (table, room) in enumerate(tables)]
    for table in tables:
        table.start()
    loads[1].wait()
    wide_mean[...] = mean[...].astype(jnp.float32)
    loads[2].wait()
    wide_square[...] = square[...].astype(jnp.float32)
    for table in tables:
        table.wait()
    loads[3].wait()
    for row in range(rows):
        base = (row // SUB) * chunks * SUB + row % SUB
        spots = pl.ds(base, chunks, stride=SUB)
        slot = slot_of[0, row]
        out_ref[slot, pl.ds(0, chunks), :] = master[spots, :].astype(jnp.bfloat16)
        out_ref[slot, pl.ds(chunks, chunks), :] = (wide_mean[spots, :] * mscale_of[0, row]).astype(jnp.bfloat16)
        out_ref[slot, pl.ds(2 * chunks, chunks), :] = (wide_square[spots, :] * sscale_of[0, row]).astype(jnp.bfloat16)


def pack(old_map, mean_scale, square_scale, master, mean, square, slot_total):
    rows, cols = master.shape
    chunks = cols // LANES
    hbm = pl.BlockSpec(memory_space=pl.ANY)
    vmem = pl.BlockSpec(memory_space=pltpu.VMEM)
    flat = (rows * chunks, LANES)
    f32, i32 = jnp.float32, jnp.int32
    block_map = old_map.reshape(-1, rows)
    return pl.pallas_call(
        functools.partial(pack_kernel, rows, chunks),
        out_shape=jax.ShapeDtypeStruct((slot_total, 3 * chunks, LANES), jnp.bfloat16),
        in_specs=[hbm, vmem, vmem, hbm, hbm, hbm],
        out_specs=vmem,
        scratch_shapes=[
            pltpu.VMEM(block_map.shape, i32),
            pltpu.VMEM(flat, f32),
            pltpu.VMEM(flat, mean.dtype),
            pltpu.VMEM(flat, square.dtype),
            pltpu.VMEM(flat, f32),
            pltpu.VMEM(flat, f32),
            pltpu.VMEM((1, rows), i32),
            pltpu.VMEM((1, rows), f32),
            pltpu.VMEM((1, rows), f32),
            pltpu.SMEM((1, rows), i32),
            pltpu.SMEM((1, rows), f32),
            pltpu.SMEM((1, rows), f32),
            pltpu.SemaphoreType.DMA((4,)),
            pltpu.SemaphoreType.DMA((3,)),
        ],
        compiler_params=pltpu.CompilerParams(vmem_limit_bytes=56 * 1024 * 1024),
        name="pack",
    )(
        block_map,
        mean_scale.reshape(1, rows),
        square_scale.reshape(1, rows),
        to_tiles(master),
        to_tiles(mean),
        to_tiles(square),
    )


def unpack_kernel(rows, chunks, slot_ref, in_ref, out_ref, weight_old, mean_old, square_old):
    span = chunks * SUB
    stages = (weight_old, mean_old, square_old)
    for group in range(rows // SUB):
        buf = group % 2
        for r in range(SUB):
            slot = slot_ref[group * SUB + r]
            spots = pl.ds(buf * span + r, chunks, stride=SUB)
            for k, stage in enumerate(stages):
                stage[spots, :] = in_ref[slot, pl.ds(k * chunks, chunks), :].astype(jnp.float32)
        for k, stage in enumerate(stages):
            out_ref[k, pl.ds(group * span, span), :] = stage[pl.ds(buf * span, span), :].astype(out_ref.dtype)


def unpack(slots, arrived, rows, chunks):
    stage = pltpu.VMEM((2 * chunks * SUB, LANES), jnp.float32)
    vmem = pl.BlockSpec(memory_space=pltpu.VMEM)
    return pl.pallas_call(
        functools.partial(unpack_kernel, rows, chunks),
        out_shape=jax.ShapeDtypeStruct((3, rows * chunks, LANES), arrived.dtype),
        in_specs=[pl.BlockSpec(memory_space=pltpu.SMEM), vmem],
        out_specs=vmem,
        scratch_shapes=[stage, stage, stage],
        compiler_params=pltpu.CompilerParams(vmem_limit_bytes=24 * 1024 * 1024),
        name="unpack",
    )(slots, arrived)


def start_loads(half, old_ref, mine_ref, side_refs, old, addends, sems):
    loads = []
    for h in range(2):
        part = pl.ds(h * half, half)
        pairs = [(mine_ref.at[part], addends.at[0, part])]
        pairs += [(side_refs[2 * k + h], addends.at[1 + k, part]) for k in range(2)]
        pairs += [(old_ref.at[k, part], old.at[k, part]) for k in range(3)]
        loads.append([pltpu.make_async_copy(ref, room, sems.at[h, k]) for k, (ref, room) in enumerate(pairs)])
    for load in loads[0] + loads[1]:
        load.start()
    return loads


def step_values(old, addends, there):
    gradient = addends[0, there, :].astype(jnp.float32)
    for k in range(1, ADDENDS):
        gradient += addends[k, there, :].astype(jnp.float32)
    weight_old, mean_old, square_old = (old[k, there, :].astype(jnp.float32) for k in range(3))
    mean_next = 0.9 * mean_old + 0.1 * gradient
    square_next = 0.95 * square_old + 0.05 * gradient * gradient
    master = weight_old - 0.05 * (mean_next / (jnp.sqrt(square_next) + 1e-08) + 0.1 * weight_old)
    return mean_next, square_next, master


def weights_kernel(rows, chunks, old_ref, mine_ref, *refs):
    side_refs, out_refs = refs[:4], refs[4:6]
    old, addends, weights, sems, out_sems = refs[6:]
    span = chunks * SUB
    groups = rows // SUB
    half = groups // 2 * span
    loads = start_loads(half, old_ref, mine_ref, side_refs, old, addends, sems)
    stores = []
    for h in range(2):
        for load in loads[h]:
            load.wait()
        for group in range(h * groups // 2, (h + 1) * groups // 2):
            there = pl.ds(group * span, span)
            weights[there, :] = step_values(old, addends, there)[2].astype(weights.dtype)
        stores.append(pltpu.make_async_copy(weights.at[pl.ds(h * half, half)], out_refs[h], out_sems.at[h]))
        stores[h].start()
    for store in stores:
        store.wait()


def new_weights(old, addends, rows, chunks):
    flat = (rows * chunks, LANES)
    bf16 = jnp.bfloat16
    hbm = pl.BlockSpec(memory_space=pl.ANY)
    return pl.pallas_call(
        functools.partial(weights_kernel, rows, chunks),
        out_shape=[jax.ShapeDtypeStruct((flat[0] // 2, LANES), bf16)] * 2,
        in_specs=[hbm] * 6,
        out_specs=[hbm] * 2,
        scratch_shapes=[
            pltpu.VMEM((3, *flat), bf16),
            pltpu.VMEM((ADDENDS, *flat), bf16),
            pltpu.VMEM(flat, bf16),
            pltpu.SemaphoreType.DMA((2, 3 + ADDENDS)),
            pltpu.SemaphoreType.DMA((2,)),
        ],
        compiler_params=pltpu.CompilerParams(vmem_limit_bytes=56 * 1024 * 1024),
        name="new_weights",
    )(old, *addends)


def adam_kernel(rows, chunks, old_ref, mine_ref, *refs):
    side_refs, weight_refs, refs = refs[:4], refs[4:6], refs[6:]
    whole_ref, master_ref, mcode_ref, scode_ref, mscale_ref, sscale_ref = refs[:6]
    old, addends, weights, sems, in_sems, out_sems = refs[6:]
    span = chunks * SUB
    groups = rows // SUB
    half = groups // 2 * span
    loads = start_loads(half, old_ref, mine_ref, side_refs, old, addends, sems)
    own = lax.axis_index("dp") * 2 * half
    fetches = [pltpu.make_async_copy(weight_refs[h], weights.at[h], in_sems.at[h]) for h in range(2)]
    stores = [
        pltpu.make_async_copy(weights.at[h], whole_ref.at[pl.ds(pl.multiple_of(own + h * half, half), half)], out_sems.at[h])
        for h in range(2)
    ]
    for fetch in fetches:
        fetch.start()
    lane = lax.broadcasted_iota(jnp.int32, (SUB, LANES), 1)
    sub = lax.broadcasted_iota(jnp.int32, (SUB, LANES), 0)
    mline = jnp.zeros((SUB, LANES), jnp.float32)
    sline = jnp.zeros((SUB, LANES), jnp.float32)
    for group in range(groups):
        if group % (groups // 2) == 0:
            h = group * 2 // groups
            for load in loads[h]:
                load.wait()
            fetches[h].wait()
            stores[h].start()
        there = pl.ds(group * span, span)
        mean_next, square_next, master = step_values(old, addends, there)
        master_ref[there, :] = master
        mean_next = mean_next.reshape(chunks, SUB, LANES)
        square_next = square_next.reshape(chunks, SUB, LANES)
        mpeak = jnp.max(jnp.max(jnp.abs(mean_next), axis=0), axis=1, keepdims=True)
        speak = jnp.max(jnp.max(square_next, axis=0), axis=1, keepdims=True)
        mscale = (mpeak + 1e-06).astype(jnp.bfloat16).astype(jnp.float32)
        sscale = (speak + 1e-06).astype(jnp.bfloat16).astype(jnp.float32)
        mcode_ref[there, :] = (mean_next * (1.0 / mscale)[None]).reshape(span, LANES).astype(jnp.bfloat16)
        scode_ref[there, :] = (square_next * (1.0 / sscale)[None]).reshape(span, LANES).astype(jnp.bfloat16)
        mine = lane == sub + group * SUB
        mline = jnp.where(mine, mscale, mline)
        sline = jnp.where(mine, sscale, sline)
    mscale_ref[...] = jnp.sum(mline, axis=0, keepdims=True).astype(jnp.bfloat16)
    sscale_ref[...] = jnp.sum(sline, axis=0, keepdims=True).astype(jnp.bfloat16)
    for store in stores:
        store.wait()


def adam(old, addends, weights, rows, chunks):
    flat = (rows * chunks, LANES)
    bf16, f32 = jnp.bfloat16, jnp.float32
    vmem = pl.BlockSpec(memory_space=pltpu.VMEM)
    return pl.pallas_call(
        functools.partial(adam_kernel, rows, chunks),
        out_shape=[
            jax.ShapeDtypeStruct((RING * CORES * flat[0], LANES), bf16),
            jax.ShapeDtypeStruct(flat, f32),
            jax.ShapeDtypeStruct(flat, bf16),
            jax.ShapeDtypeStruct(flat, bf16),
            jax.ShapeDtypeStruct((1, rows), bf16),
            jax.ShapeDtypeStruct((1, rows), bf16),
        ],
        in_specs=[pl.BlockSpec(memory_space=pl.ANY)] * 8,
        out_specs=[pl.BlockSpec(memory_space=pl.ANY)] + [vmem] * 5,
        scratch_shapes=[
            pltpu.VMEM((3, *flat), bf16),
            pltpu.VMEM((ADDENDS, *flat), bf16),
            pltpu.VMEM((2, flat[0] // 2, LANES), bf16),
            pltpu.SemaphoreType.DMA((2, 3 + ADDENDS)),
            pltpu.SemaphoreType.DMA((2,)),
            pltpu.SemaphoreType.DMA((2,)),
        ],
        compiler_params=pltpu.CompilerParams(vmem_limit_bytes=56 * 1024 * 1024),
        cost_estimate=pl.CostEstimate(flops=0, transcendentals=0, bytes_accessed=16 * 1024 * 1024),
        name="adam",
    )(old, *addends, *weights)


def place():
    me = lax.axis_index("dp")
    return me // CORES, me % CORES


def shard_at(y, step, core):
    return lax.rem(y + step, RING) * CORES + core


def sends(shift, flip):
    return [
        (y * CORES + c, (y + shift) % RING * CORES + (CORES - 1 - c if flip else c))
        for y in range(RING)
        for c in range(CORES)
    ]


def send(values, shift, flip=False, name="r_send"):
    with jax.named_scope(name):
        return lax.ppermute(values, "dp", sends(shift, flip))


def cut_kernel(shards, grad_ref, *refs):
    out_refs, (room, in_sems, out_sems) = refs[: len(shards)], refs[len(shards) :]
    y, core = place()
    loads, stores = [], []
    for k, (step, flip) in enumerate(shards):
        shard = shard_at(y, step, CORES - 1 - core if flip else core)
        loads.append(pltpu.make_async_copy(grad_ref.at[shard], room.at[k], in_sems.at[k]))
        stores.append(pltpu.make_async_copy(room.at[k], out_refs[k], out_sems.at[k]))
    for load in loads:
        load.start()
    for load, store in zip(loads, stores):
        load.wait()
        store.start()
    for store in stores:
        store.wait()


def cut(grads, shards):
    _, span, lanes = grads.shape
    count = len(shards)
    hbm = pl.BlockSpec(memory_space=pl.ANY)
    return pl.pallas_call(
        functools.partial(cut_kernel, shards),
        out_shape=[jax.ShapeDtypeStruct((span, lanes), grads.dtype)] * count,
        in_specs=[hbm],
        out_specs=[hbm] * count,
        scratch_shapes=[pltpu.VMEM((count, span, lanes), grads.dtype)] + [pltpu.SemaphoreType.DMA((count,))] * 2,
        compiler_params=pltpu.CompilerParams(vmem_limit_bytes=56 * 1024 * 1024),
        name="cut",
    )(grads)


def add_kernel(windows, sums, *refs):
    count, outs = len(windows), len(sums)
    in_refs, out_refs, rooms, totals = refs[:count], refs[count:][:outs], refs[count + outs :][:count], refs[2 * count + outs : -2]
    in_sems, out_sems = refs[-2:]
    loads = [
        pltpu.make_async_copy(ref.at[pl.ds(*window)], room, in_sems.at[k])
        for k, (ref, window, room) in enumerate(zip(in_refs, windows, rooms))
    ]
    for load in loads:
        load.start()
    stores = []
    for k, terms in enumerate(sums):
        total = None
        for term in terms:
            loads[term].wait()
            values = rooms[term][...].astype(jnp.float32)
            total = values if total is None else total + values
        totals[k][...] = total.astype(totals[k].dtype)
        store = pltpu.make_async_copy(totals[k], out_refs[k], out_sems.at[k])
        store.start()
        stores.append(store)
    for store in stores:
        store.wait()


def add(*sums):
    terms = [term for parts in sums for term in parts]
    lanes, dtype = terms[0][0].shape[1], terms[0][0].dtype
    hbm = pl.BlockSpec(memory_space=pl.ANY)
    order, at = [], 0
    for parts in sums:
        order.append(tuple(range(at, at + len(parts))))
        at += len(parts)
    windows = [(first, rows) for _, first, rows in terms]
    shapes = [(rows, lanes) for _, rows in windows]
    outs = [(parts[0][2], lanes) for parts in sums]
    return pl.pallas_call(
        functools.partial(add_kernel, windows, order),
        out_shape=[jax.ShapeDtypeStruct(shape, dtype) for shape in outs],
        in_specs=[hbm] * len(terms),
        out_specs=[hbm] * len(outs),
        scratch_shapes=[pltpu.VMEM(shape, dtype) for shape in shapes + outs]
        + [pltpu.SemaphoreType.DMA((len(terms),)), pltpu.SemaphoreType.DMA((len(outs),))],
        compiler_params=pltpu.CompilerParams(vmem_limit_bytes=56 * 1024 * 1024),
        name="add",
    )(*[array for array, _, _ in terms])


def reduce_shards(grads, arrived):
    span = grads.shape[1]
    half = span // 2
    steps = (2, 1, 3, 0)
    got = dict(zip(steps, [send(part, 0, True) for part in cut(grads, tuple((step, 1) for step in steps))]))
    own = dict(zip(steps, cut(grads, tuple((step, 0) for step in steps))))

    def both(step, first, rows):
        return [(own[step], first, rows), (got[step], first, rows)]

    opp_lo, opp_hi, up_hi, dn_lo, mine = add(
        both(2, 0, half), both(2, half, half), both(1, half, half), both(3, 0, half), both(0, 0, span)
    )
    opp_up, opp_dn = send(opp_lo, 1), send(opp_hi, 3)
    up_hi_got, dn_lo_got = send(up_hi, 1), send(dn_lo, 3)
    opp_up, opp_dn, arrived = lax.optimization_barrier((opp_up, opp_dn, arrived))
    up_lo, dn_hi = add(both(1, 0, half) + [(opp_up, 0, half)], both(3, half, half) + [(opp_dn, 0, half)])
    return (mine, send(up_lo, 1), up_hi_got, dn_lo_got, send(dn_hi, 3)), arrived


def join_kernel(span, starts, *refs):
    parts, (out_ref, *rooms, in_sems, sems) = refs[: len(starts)], refs[-3 - len(starts) :]
    y, core = place()
    loads = [pltpu.make_async_copy(part, room, in_sems.at[k]) for k, (part, room) in enumerate(zip(parts, rooms))]
    for load in loads:
        load.start()
    copies = []
    for k, (step, flip, offset) in enumerate(starts):
        side = CORES - 1 - core if flip else core
        base = pl.multiple_of(shard_at(y, step, side) * span + offset, span // 2)
        copies.append(pltpu.make_async_copy(rooms[k], out_ref.at[pl.ds(base, parts[k].shape[0])], sems.at[k]))
    for load, copy in zip(loads, copies):
        load.wait()
        copy.start()
    for copy in copies:
        copy.wait()


def join(span, starts, parts, whole=None):
    lanes = parts[0].shape[1]
    hbm = pl.BlockSpec(memory_space=pl.ANY)
    given = list(parts) + ([] if whole is None else [whole])
    return pl.pallas_call(
        functools.partial(join_kernel, span, starts),
        out_shape=jax.ShapeDtypeStruct((RING * CORES * span, lanes), parts[0].dtype),
        in_specs=[hbm] * len(given),
        out_specs=hbm,
        scratch_shapes=[pltpu.VMEM(part.shape, part.dtype) for part in parts]
        + [pltpu.SemaphoreType.DMA((len(parts),))] * 2,
        compiler_params=pltpu.CompilerParams(vmem_limit_bytes=16 * 1024 * 1024),
        input_output_aliases={} if whole is None else {len(parts): 0},
        cost_estimate=pl.CostEstimate(flops=0, transcendentals=0, bytes_accessed=0),
        name="join",
    )(*given)


def gather_shards(lo, hi, run_between):
    half = lo.shape[0]
    span = 2 * half
    up_lo, dn_hi = send(lo, 1, name="g_up_lo"), send(hi, 3, name="g_dn_hi")
    up_hi, dn_lo = send(hi, 1, name="g_up_hi"), send(lo, 3, name="g_dn_lo")
    sib_lo, sib_hi = send(lo, 0, True, name="g_sib_lo"), send(hi, 0, True, name="g_sib_hi")
    whole, *rest = run_between(sib_lo)
    up_lo, dn_hi, rest[-1] = lax.optimization_barrier((up_lo, dn_hi, rest[-1]))
    opp_lo, opp_hi = send(up_lo, 1, name="g_opp_lo"), send(dn_hi, 3, name="g_opp_hi")
    sib_up_lo, sib_dn_hi = send(up_lo, 0, True, name="g_sib_up_lo"), send(dn_hi, 0, True, name="g_sib_dn_hi")
    starts = [(3, 0, 0), (1, 0, half), (3, 0, half), (1, 0, 0), (0, 1, 0), (0, 1, half)]
    whole = join(span, starts, [up_lo, dn_hi, up_hi, dn_lo, sib_lo, sib_hi], whole)
    whole, up_hi, dn_lo, opp_lo, opp_hi = lax.optimization_barrier((whole, up_hi, dn_lo, opp_lo, opp_hi))
    parts = [opp_lo, opp_hi]
    for part, name in zip((opp_lo, opp_hi, up_hi, dn_lo), ("opp_lo", "opp_hi", "up_hi", "dn_lo")):
        parts.append(send(part, 0, True, name="g_sib_" + name))
    parts += [sib_up_lo, sib_dn_hi]
    starts = [(2, 0, 0), (2, 0, half), (2, 1, 0), (2, 1, half), (3, 1, half), (1, 1, 0), (3, 1, 0), (1, 1, half)]
    return join(span, starts, parts, whole), rest


def arrivals(old_map, block_rows, peer_cap):
    self_index = lax.axis_index(ALL)
    wanted = lax.dynamic_slice_in_dim(old_map, self_index * block_rows, block_rows)
    source = wanted // block_rows
    return source * peer_cap + pair_rank(source, jnp.arange(block_rows, dtype=jnp.int32))


def local(grad_parts, old_master, old_mean, old_mean_scale, old_square, old_square_scale, old_map):
    count_all = lax.axis_size(ALL)
    block_rows, block_len = old_master.shape
    peer_cap = 2
    slot_total = count_all * peer_cap
    chunks = block_len // LANES
    grads = to_tiles(grad_parts[0]).reshape(RING * CORES, block_rows * chunks, LANES)
    packed = pack(old_map, old_mean_scale, old_square_scale, old_master, old_mean, old_square, slot_total)
    packed, late_grads, late_map = lax.optimization_barrier((packed, grads, old_map))
    arrived = lax.all_to_all(
        packed.reshape(count_all, peer_cap * 3 * chunks, LANES), ALL, split_axis=0, concat_axis=0, tiled=True
    ).reshape(slot_total, 3 * chunks, LANES)
    addends, arrived = reduce_shards(late_grads, arrived)
    old = unpack(arrivals(late_map, block_rows, peer_cap), arrived, block_rows, chunks)
    lo, hi = new_weights(old, addends, block_rows, chunks)

    def run_between(*arrived_first):
        late_old, late_addends, _ = lax.optimization_barrier((old, addends, arrived_first))
        return adam(late_old, late_addends, (lo, hi), block_rows, chunks)

    weights, rest = gather_shards(lo, hi, run_between)
    *blocks, mean_scales, square_scales = rest
    master, mean_codes, square_codes = (from_tiles(x, block_rows, block_len) for x in blocks)
    weights = from_tiles(weights, RING * CORES * block_rows, block_len)
    return (weights, master, mean_codes, mean_scales.reshape(-1), square_codes, square_scales.reshape(-1))


def solution(mesh):
    in_specs = (
        P("dp", "fsdp", None),
        P(ALL, None),
        P(ALL, None),
        P(ALL),
        P(ALL, None),
        P(ALL),
        P(),
    )
    out_specs = (
        P("fsdp", None),
        P(ALL, None),
        P(ALL, None),
        P(ALL),
        P(ALL, None),
        P(ALL),
    )
    return jax.shard_map(local, mesh=mesh, in_specs=in_specs, out_specs=out_specs, check_vma=False)
```

```python
import functools

import jax
import jax.numpy as jnp
from jax import lax
from jax.experimental import pallas as pl
from jax.experimental.pallas import tpu as pltpu
from jax.sharding import PartitionSpec as P

ALL = ("fsdp", "dp")
LANES = 128
SUB = 8
RING = 4
CORES = 2
ADDENDS = 3
STRIP = 32


def to_tiles(values):
    rows, cols = values.shape
    tiled = values.reshape(rows // SUB, SUB, cols // LANES, LANES)
    return tiled.transpose(0, 2, 1, 3).reshape(rows * cols // LANES, LANES)


def from_tiles(values, rows, cols):
    tiled = values.reshape(rows // SUB, cols // LANES, SUB, LANES)
    return tiled.transpose(0, 2, 1, 3).reshape(rows, cols)


def pair_rank(owners, keyed):
    matching = owners[:, None] == owners[None, :]
    before = keyed[None, :] < keyed[:, None]
    return jnp.sum(jnp.where(matching & before, 1, 0), axis=1).astype(jnp.int32)


def send_slots(block_map, rows):
    owners = block_map.shape[0]
    first_slot = (lax.axis_index("fsdp") * lax.axis_size("dp") + lax.axis_index("dp")) * rows
    held = block_map - first_slot
    here = (held >= 0) & (held < rows)
    spot = lax.broadcasted_iota(jnp.int32, block_map.shape, 1)
    first = jnp.min(jnp.where(here, spot, rows), axis=1, keepdims=True)
    one = jnp.max(jnp.where(here & (spot == first), held, -1), axis=1, keepdims=True)
    two = jnp.max(jnp.where(here & (spot > first), held, -1), axis=1, keepdims=True)
    owner = lax.broadcasted_iota(jnp.int32, (owners, rows), 0)
    slot = lax.broadcasted_iota(jnp.int32, (owners, rows), 1)
    place_of = jnp.where(one == slot, 2 * owner, 0) + jnp.where(two == slot, 2 * owner + 1, 0)
    return jnp.sum(place_of, axis=0, keepdims=True)


def pack_kernel(rows, chunks, map_ref, mscale_ref, sscale_ref, master_ref, mean_ref, square_ref, out_ref, *scratch):
    held_map, master, mean, square, wide_mean, wide_square, slots, mscale, sscale, slot_of, mscale_of, sscale_of = scratch[:12]
    load_sems, table_sems = scratch[12:]
    part = rows * chunks // 2
    pairs = [(map_ref, held_map)]
    for h in range(2):
        here = pl.ds(h * part, part)
        pairs += [(ref.at[here], room.at[here]) for ref, room in ((mean_ref, mean), (square_ref, square), (master_ref, master))]
    loads = [pltpu.make_async_copy(ref, room, load_sems.at[k]) for k, (ref, room) in enumerate(pairs)]
    for load in loads:
        load.start()
    mscale[...] = mscale_ref[...].astype(jnp.float32)
    sscale[...] = sscale_ref[...].astype(jnp.float32)
    loads[0].wait()
    slots[...] = send_slots(held_map[...], rows)
    tables = [(slots, slot_of), (mscale, mscale_of), (sscale, sscale_of)]
    tables = [pltpu.make_async_copy(table, room, table_sems.at[k]) for k, (table, room) in enumerate(tables)]
    for table in tables:
        table.start()
    for row in range(rows):
        if row % (rows // 2) == 0:
            first = 1 + 3 * (row * 2 // rows)
            here = pl.ds(row * chunks, part)
            loads[first].wait()
            wide_mean[here, :] = mean[here, :].astype(jnp.float32)
            loads[first + 1].wait()
            wide_square[here, :] = square[here, :].astype(jnp.float32)
            loads[first + 2].wait()
        if row == 0:
            for table in tables:
                table.wait()
        base = (row // SUB) * chunks * SUB + row % SUB
        spots = pl.ds(base, chunks, stride=SUB)
        slot = slot_of[0, row]
        out_ref[slot, pl.ds(0, chunks), :] = master[spots, :].astype(jnp.bfloat16)
        out_ref[slot, pl.ds(chunks, chunks), :] = (wide_mean[spots, :] * mscale_of[0, row]).astype(jnp.bfloat16)
        out_ref[slot, pl.ds(2 * chunks, chunks), :] = (wide_square[spots, :] * sscale_of[0, row]).astype(jnp.bfloat16)


def pack(old_map, mean_scale, square_scale, master, mean, square, slot_total):
    rows, cols = master.shape
    chunks = cols // LANES
    hbm = pl.BlockSpec(memory_space=pl.ANY)
    vmem = pl.BlockSpec(memory_space=pltpu.VMEM)
    flat = (rows * chunks, LANES)
    f32, i32 = jnp.float32, jnp.int32
    block_map = old_map.reshape(-1, rows)
    return pl.pallas_call(
        functools.partial(pack_kernel, rows, chunks),
        out_shape=jax.ShapeDtypeStruct((slot_total, 3 * chunks, LANES), jnp.bfloat16),
        in_specs=[hbm, vmem, vmem, hbm, hbm, hbm],
        out_specs=vmem,
        scratch_shapes=[
            pltpu.VMEM(block_map.shape, i32),
            pltpu.VMEM(flat, f32),
            pltpu.VMEM(flat, mean.dtype),
            pltpu.VMEM(flat, square.dtype),
            pltpu.VMEM(flat, f32),
            pltpu.VMEM(flat, f32),
            pltpu.VMEM((1, rows), i32),
            pltpu.VMEM((1, rows), f32),
            pltpu.VMEM((1, rows), f32),
            pltpu.SMEM((1, rows), i32),
            pltpu.SMEM((1, rows), f32),
            pltpu.SMEM((1, rows), f32),
            pltpu.SemaphoreType.DMA((7,)),
            pltpu.SemaphoreType.DMA((3,)),
        ],
        compiler_params=pltpu.CompilerParams(vmem_limit_bytes=56 * 1024 * 1024),
        name="pack",
    )(
        block_map,
        mean_scale.reshape(1, rows),
        square_scale.reshape(1, rows),
        to_tiles(master),
        to_tiles(mean),
        to_tiles(square),
    )


def unpack_kernel(rows, chunks, slot_ref, in_ref, out_ref, weight_old, mean_old, square_old):
    span = chunks * SUB
    stages = (weight_old, mean_old, square_old)
    for group in range(rows // SUB):
        buf = group % 2
        for r in range(SUB):
            slot = slot_ref[group * SUB + r]
            spots = pl.ds(buf * span + r, chunks, stride=SUB)
            for k, stage in enumerate(stages):
                stage[spots, :] = in_ref[slot, pl.ds(k * chunks, chunks), :].astype(jnp.float32)
        for k, stage in enumerate(stages):
            out_ref[k, pl.ds(group * span, span), :] = stage[pl.ds(buf * span, span), :].astype(out_ref.dtype)


def unpack(slots, arrived, rows, chunks):
    stage = pltpu.VMEM((2 * chunks * SUB, LANES), jnp.float32)
    vmem = pl.BlockSpec(memory_space=pltpu.VMEM)
    return pl.pallas_call(
        functools.partial(unpack_kernel, rows, chunks),
        out_shape=jax.ShapeDtypeStruct((3, rows * chunks, LANES), arrived.dtype),
        in_specs=[pl.BlockSpec(memory_space=pltpu.SMEM), vmem],
        out_specs=vmem,
        scratch_shapes=[stage, stage, stage],
        compiler_params=pltpu.CompilerParams(vmem_limit_bytes=24 * 1024 * 1024),
        name="unpack",
    )(slots, arrived)


def start_loads(half, old_ref, mine_ref, side_refs, old, addends, sems):
    loads = []
    for h in range(2):
        part = pl.ds(h * half, half)
        pairs = [(mine_ref.at[part], addends.at[0, part])]
        pairs += [(side_refs[2 * k + h], addends.at[1 + k, part]) for k in range(2)]
        pairs += [(old_ref.at[k, part], old.at[k, part]) for k in range(3)]
        loads.append([pltpu.make_async_copy(ref, room, sems.at[h, k]) for k, (ref, room) in enumerate(pairs)])
    for load in loads[0] + loads[1]:
        load.start()
    return loads


def step_values(old, gradient):
    weight_old, mean_old, square_old = (x.astype(jnp.float32) for x in old)
    mean_next = 0.9 * mean_old + 0.1 * gradient
    square_next = 0.95 * square_old + 0.05 * gradient * gradient
    root = square_next * lax.rsqrt(square_next)
    master = weight_old - 0.05 * (mean_next / (root + 1e-08) + 0.1 * weight_old)
    return mean_next, square_next, master


def weights_kernel(old_ref, mine_ref, *refs):
    side_refs, out_refs = refs[:4], refs[4:]
    half = out_refs[0].shape[0]
    for h in range(2):
        for start in range(0, half, STRIP):
            there, inside = pl.ds(h * half + start, STRIP), pl.ds(start, STRIP)
            gradient = mine_ref[there, :].astype(jnp.float32)
            for side in range(2):
                gradient += side_refs[2 * side + h][inside, :].astype(jnp.float32)
            master = step_values([old_ref[k, there, :] for k in range(3)], gradient)[2]
            out_refs[h][inside, :] = master.astype(out_refs[h].dtype)


def new_weights(old, addends, rows, chunks):
    vmem = pl.BlockSpec(memory_space=pltpu.VMEM)
    return pl.pallas_call(
        weights_kernel,
        out_shape=[jax.ShapeDtypeStruct((rows * chunks // 2, LANES), jnp.bfloat16)] * 2,
        in_specs=[vmem] * 6,
        out_specs=[vmem] * 2,
        compiler_params=pltpu.CompilerParams(vmem_limit_bytes=12 * 1024 * 1024),
        name="new_weights",
    )(old, *addends)


def adam_kernel(rows, chunks, old_ref, mine_ref, *refs):
    side_refs, weight_refs, refs = refs[:4], refs[4:6], refs[6:]
    whole_ref, master_ref, mcode_ref, scode_ref, mscale_ref, sscale_ref = refs[:6]
    old, addends, weights, sems, in_sems, out_sems = refs[6:]
    span = chunks * SUB
    groups = rows // SUB
    half = groups // 2 * span
    loads = start_loads(half, old_ref, mine_ref, side_refs, old, addends, sems)
    own = lax.axis_index("dp") * 2 * half
    fetches = [pltpu.make_async_copy(weight_refs[h], weights.at[h], in_sems.at[h]) for h in range(2)]
    stores = [
        pltpu.make_async_copy(weights.at[h], whole_ref.at[pl.ds(pl.multiple_of(own + h * half, half), half)], out_sems.at[h])
        for h in range(2)
    ]
    for fetch in fetches:
        fetch.start()
    lane = lax.broadcasted_iota(jnp.int32, (SUB, LANES), 1)
    sub = lax.broadcasted_iota(jnp.int32, (SUB, LANES), 0)
    mline = jnp.zeros((SUB, LANES), jnp.float32)
    sline = jnp.zeros((SUB, LANES), jnp.float32)
    for group in range(groups):
        if group % (groups // 2) == 0:
            h = group * 2 // groups
            for load in loads[h]:
                load.wait()
            fetches[h].wait()
            stores[h].start()
        there = pl.ds(group * span, span)
        gradient = addends[0, there, :].astype(jnp.float32)
        for k in range(1, ADDENDS):
            gradient += addends[k, there, :].astype(jnp.float32)
        mean_next, square_next, master = step_values([old[k, there, :] for k in range(3)], gradient)
        master_ref[there, :] = master
        mean_next = mean_next.reshape(chunks, SUB, LANES)
        square_next = square_next.reshape(chunks, SUB, LANES)
        mpeak = jnp.max(jnp.max(jnp.abs(mean_next), axis=0), axis=1, keepdims=True)
        speak = jnp.max(jnp.max(square_next, axis=0), axis=1, keepdims=True)
        mscale = (mpeak + 1e-06).astype(jnp.bfloat16).astype(jnp.float32)
        sscale = (speak + 1e-06).astype(jnp.bfloat16).astype(jnp.float32)
        mcode_ref[there, :] = (mean_next * (1.0 / mscale)[None]).reshape(span, LANES).astype(jnp.bfloat16)
        scode_ref[there, :] = (square_next * (1.0 / sscale)[None]).reshape(span, LANES).astype(jnp.bfloat16)
        mine = lane == sub + group * SUB
        mline = jnp.where(mine, mscale, mline)
        sline = jnp.where(mine, sscale, sline)
    mscale_ref[...] = jnp.sum(mline, axis=0, keepdims=True).astype(jnp.bfloat16)
    sscale_ref[...] = jnp.sum(sline, axis=0, keepdims=True).astype(jnp.bfloat16)
    for store in stores:
        store.wait()


def adam(old, addends, weights, rows, chunks):
    flat = (rows * chunks, LANES)
    bf16, f32 = jnp.bfloat16, jnp.float32
    vmem = pl.BlockSpec(memory_space=pltpu.VMEM)
    return pl.pallas_call(
        functools.partial(adam_kernel, rows, chunks),
        out_shape=[
            jax.ShapeDtypeStruct((RING * CORES * flat[0], LANES), bf16),
            jax.ShapeDtypeStruct(flat, f32),
            jax.ShapeDtypeStruct(flat, bf16),
            jax.ShapeDtypeStruct(flat, bf16),
            jax.ShapeDtypeStruct((1, rows), bf16),
            jax.ShapeDtypeStruct((1, rows), bf16),
        ],
        in_specs=[pl.BlockSpec(memory_space=pl.ANY)] * 8,
        out_specs=[pl.BlockSpec(memory_space=pl.ANY)] + [vmem] * 5,
        scratch_shapes=[
            pltpu.VMEM((3, *flat), bf16),
            pltpu.VMEM((ADDENDS, *flat), bf16),
            pltpu.VMEM((2, flat[0] // 2, LANES), bf16),
            pltpu.SemaphoreType.DMA((2, 3 + ADDENDS)),
            pltpu.SemaphoreType.DMA((2,)),
            pltpu.SemaphoreType.DMA((2,)),
        ],
        compiler_params=pltpu.CompilerParams(vmem_limit_bytes=56 * 1024 * 1024),
        cost_estimate=pl.CostEstimate(flops=0, transcendentals=0, bytes_accessed=16 * 1024 * 1024),
        name="adam",
    )(old, *addends, *weights)


def place():
    me = lax.axis_index("dp")
    return me // CORES, me % CORES


def shard_at(y, step, core):
    return lax.rem(y + step, RING) * CORES + core


def sends(shift, flip):
    return [
        (y * CORES + c, (y + shift) % RING * CORES + (CORES - 1 - c if flip else c))
        for y in range(RING)
        for c in range(CORES)
    ]


def send(values, shift, flip=False, name="r_send"):
    with jax.named_scope(name):
        return lax.ppermute(values, "dp", sends(shift, flip))


def cut_kernel(shards, grad_ref, *refs):
    out_refs, (room, in_sems, out_sems) = refs[: len(shards)], refs[len(shards) :]
    y, core = place()
    loads, stores = [], []
    for k, (step, flip) in enumerate(shards):
        shard = shard_at(y, step, CORES - 1 - core if flip else core)
        loads.append(pltpu.make_async_copy(grad_ref.at[shard], room.at[k], in_sems.at[k]))
        stores.append(pltpu.make_async_copy(room.at[k], out_refs[k], out_sems.at[k]))
    for load in loads:
        load.start()
    for load, store in zip(loads, stores):
        load.wait()
        store.start()
    for store in stores:
        store.wait()


def cut(grads, shards):
    _, span, lanes = grads.shape
    count = len(shards)
    hbm = pl.BlockSpec(memory_space=pl.ANY)
    return pl.pallas_call(
        functools.partial(cut_kernel, shards),
        out_shape=[jax.ShapeDtypeStruct((span, lanes), grads.dtype)] * count,
        in_specs=[hbm],
        out_specs=[hbm] * count,
        scratch_shapes=[pltpu.VMEM((count, span, lanes), grads.dtype)] + [pltpu.SemaphoreType.DMA((count,))] * 2,
        compiler_params=pltpu.CompilerParams(vmem_limit_bytes=56 * 1024 * 1024),
        name="cut",
    )(grads)


def add_kernel(windows, sums, *refs):
    count, outs = len(windows), len(sums)
    in_refs, out_refs, rooms, totals = refs[:count], refs[count:][:outs], refs[count + outs :][:count], refs[2 * count + outs : -2]
    in_sems, out_sems = refs[-2:]
    loads = [
        pltpu.make_async_copy(ref.at[pl.ds(*window)], room, in_sems.at[k])
        for k, (ref, window, room) in enumerate(zip(in_refs, windows, rooms))
    ]
    for load in loads:
        load.start()
    stores = []
    for k, terms in enumerate(sums):
        total = None
        for term in terms:
            loads[term].wait()
            values = rooms[term][...].astype(jnp.float32)
            total = values if total is None else total + values
        totals[k][...] = total.astype(totals[k].dtype)
        store = pltpu.make_async_copy(totals[k], out_refs[k], out_sems.at[k])
        store.start()
        stores.append(store)
    for store in stores:
        store.wait()


def add(*sums):
    terms = [term for parts in sums for term in parts]
    lanes, dtype = terms[0][0].shape[1], terms[0][0].dtype
    hbm = pl.BlockSpec(memory_space=pl.ANY)
    order, at = [], 0
    for parts in sums:
        order.append(tuple(range(at, at + len(parts))))
        at += len(parts)
    windows = [(first, rows) for _, first, rows in terms]
    shapes = [(rows, lanes) for _, rows in windows]
    outs = [(parts[0][2], lanes) for parts in sums]
    return pl.pallas_call(
        functools.partial(add_kernel, windows, order),
        out_shape=[jax.ShapeDtypeStruct(shape, dtype) for shape in outs],
        in_specs=[hbm] * len(terms),
        out_specs=[hbm] * len(outs),
        scratch_shapes=[pltpu.VMEM(shape, dtype) for shape in shapes + outs]
        + [pltpu.SemaphoreType.DMA((len(terms),)), pltpu.SemaphoreType.DMA((len(outs),))],
        compiler_params=pltpu.CompilerParams(vmem_limit_bytes=56 * 1024 * 1024),
        name="add",
    )(*[array for array, _, _ in terms])


def reduce_shards(grads, arrived):
    span = grads.shape[1]
    half = span // 2
    steps = (2, 1, 3, 0)
    got = dict(zip(steps, [send(part, 0, True) for part in cut(grads, tuple((step, 1) for step in steps))]))
    own = dict(zip(steps, cut(grads, tuple((step, 0) for step in steps))))

    def both(step, first, rows):
        return [(own[step], first, rows), (got[step], first, rows)]

    opp_lo, opp_hi, up_hi, dn_lo, mine = add(
        both(2, 0, half), both(2, half, half), both(1, half, half), both(3, 0, half), both(0, 0, span)
    )
    opp_up, opp_dn = send(opp_lo, 1), send(opp_hi, 3)
    up_hi_got, dn_lo_got = send(up_hi, 1), send(dn_lo, 3)
    opp_up, opp_dn, arrived = lax.optimization_barrier((opp_up, opp_dn, arrived))
    up_lo, dn_hi = add(both(1, 0, half) + [(opp_up, 0, half)], both(3, half, half) + [(opp_dn, 0, half)])
    return (mine, send(up_lo, 1), up_hi_got, dn_lo_got, send(dn_hi, 3)), arrived


def join_kernel(span, starts, *refs):
    parts, (out_ref, sems) = refs[: len(starts)], refs[-2:]
    y, core = place()
    copies = []
    for k, (step, flip, offset) in enumerate(starts):
        side = CORES - 1 - core if flip else core
        base = pl.multiple_of(shard_at(y, step, side) * span + offset, span // 2)
        copies.append(pltpu.make_async_copy(parts[k], out_ref.at[pl.ds(base, parts[k].shape[0])], sems.at[k]))
    for copy in copies:
        copy.start()
    for copy in copies:
        copy.wait()


def join(span, starts, parts, whole):
    return pl.pallas_call(
        functools.partial(join_kernel, span, starts),
        out_shape=jax.ShapeDtypeStruct(whole.shape, whole.dtype),
        in_specs=[pl.BlockSpec(memory_space=pltpu.VMEM)] * len(parts) + [pl.BlockSpec(memory_space=pl.ANY)],
        out_specs=pl.BlockSpec(memory_space=pl.ANY),
        scratch_shapes=[pltpu.SemaphoreType.DMA((len(parts),))],
        compiler_params=pltpu.CompilerParams(vmem_limit_bytes=8 * 1024 * 1024),
        input_output_aliases={len(parts): 0},
        name="join",
    )(*parts, whole)


def gather_shards(lo, hi, run_between):
    half = lo.shape[0]
    span = 2 * half
    up_lo, dn_hi = send(lo, 1, name="g_up_lo"), send(hi, 3, name="g_dn_hi")
    up_hi, dn_lo = send(hi, 1, name="g_up_hi"), send(lo, 3, name="g_dn_lo")
    sib_lo, sib_hi = send(lo, 0, True, name="g_sib_lo"), send(hi, 0, True, name="g_sib_hi")
    whole, *rest = run_between(sib_lo)
    up_lo, dn_hi, rest[-1] = lax.optimization_barrier((up_lo, dn_hi, rest[-1]))
    opp_lo, opp_hi = send(up_lo, 1, name="g_opp_lo"), send(dn_hi, 3, name="g_opp_hi")
    sib_up_lo, sib_dn_hi = send(up_lo, 0, True, name="g_sib_up_lo"), send(dn_hi, 0, True, name="g_sib_dn_hi")
    starts = [(3, 0, 0), (1, 0, half), (3, 0, half), (1, 0, 0), (0, 1, 0), (0, 1, half)]
    whole = join(span, starts, [up_lo, dn_hi, up_hi, dn_lo, sib_lo, sib_hi], whole)
    whole, up_hi, dn_lo, opp_lo, opp_hi = lax.optimization_barrier((whole, up_hi, dn_lo, opp_lo, opp_hi))
    parts = [opp_lo, opp_hi]
    for part, name in zip((opp_lo, opp_hi, up_hi, dn_lo), ("opp_lo", "opp_hi", "up_hi", "dn_lo")):
        parts.append(send(part, 0, True, name="g_sib_" + name))
    parts += [sib_up_lo, sib_dn_hi]
    starts = [(2, 0, 0), (2, 0, half), (2, 1, 0), (2, 1, half), (3, 1, half), (1, 1, 0), (3, 1, 0), (1, 1, half)]
    return join(span, starts, parts, whole), rest


def arrivals(old_map, block_rows, peer_cap):
    self_index = lax.axis_index(ALL)
    wanted = lax.dynamic_slice_in_dim(old_map, self_index * block_rows, block_rows)
    source = wanted // block_rows
    return source * peer_cap + pair_rank(source, jnp.arange(block_rows, dtype=jnp.int32))


def local(grad_parts, old_master, old_mean, old_mean_scale, old_square, old_square_scale, old_map):
    count_all = lax.axis_size(ALL)
    block_rows, block_len = old_master.shape
    peer_cap = 2
    slot_total = count_all * peer_cap
    chunks = block_len // LANES
    grads = to_tiles(grad_parts[0]).reshape(RING * CORES, block_rows * chunks, LANES)
    packed = pack(old_map, old_mean_scale, old_square_scale, old_master, old_mean, old_square, slot_total)
    packed, late_grads, late_map = lax.optimization_barrier((packed, grads, old_map))
    arrived = lax.all_to_all(
        packed.reshape(count_all, peer_cap * 3 * chunks, LANES), ALL, split_axis=0, concat_axis=0, tiled=True
    ).reshape(slot_total, 3 * chunks, LANES)
    addends, arrived = reduce_shards(late_grads, arrived)
    old = unpack(arrivals(late_map, block_rows, peer_cap), arrived, block_rows, chunks)
    lo, hi = new_weights(old, addends, block_rows, chunks)

    def run_between(*arrived_first):
        late_old, late_addends, _ = lax.optimization_barrier((old, addends, arrived_first))
        return adam(late_old, late_addends, (lo, hi), block_rows, chunks)

    weights, rest = gather_shards(lo, hi, run_between)
    *blocks, mean_scales, square_scales = rest
    master, mean_codes, square_codes = (from_tiles(x, block_rows, block_len) for x in blocks)
    weights = from_tiles(weights, RING * CORES * block_rows, block_len)
    return (weights, master, mean_codes, mean_scales.reshape(-1), square_codes, square_scales.reshape(-1))


def solution(mesh):
    in_specs = (
        P("dp", "fsdp", None),
        P(ALL, None),
        P(ALL, None),
        P(ALL),
        P(ALL, None),
        P(ALL),
        P(),
    )
    out_specs = (
        P("fsdp", None),
        P(ALL, None),
        P(ALL, None),
        P(ALL),
        P(ALL, None),
        P(ALL),
    )
    return jax.shard_map(local, mesh=mesh, in_specs=in_specs, out_specs=out_specs, check_vma=False)
```

```python
import functools

import jax
import jax.numpy as jnp
from jax import lax
from jax.experimental import pallas as pl
from jax.experimental.pallas import tpu as pltpu
from jax.sharding import PartitionSpec as P

ALL = ("fsdp", "dp")
LANES = 128
SUB = 8
RING = 4
CORES = 2
ADDENDS = 3
STRIP = 32


def to_tiles(values):
    rows, cols = values.shape
    tiled = values.reshape(rows // SUB, SUB, cols // LANES, LANES)
    return tiled.transpose(0, 2, 1, 3).reshape(rows * cols // LANES, LANES)


def from_tiles(values, rows, cols):
    tiled = values.reshape(rows // SUB, cols // LANES, SUB, LANES)
    return tiled.transpose(0, 2, 1, 3).reshape(rows, cols)


def pair_rank(owners, keyed):
    matching = owners[:, None] == owners[None, :]
    before = keyed[None, :] < keyed[:, None]
    return jnp.sum(jnp.where(matching & before, 1, 0), axis=1).astype(jnp.int32)


def send_slots(block_map, rows):
    owners = block_map.shape[0]
    first_slot = (lax.axis_index("fsdp") * lax.axis_size("dp") + lax.axis_index("dp")) * rows
    held = block_map - first_slot
    here = (held >= 0) & (held < rows)
    spot = lax.broadcasted_iota(jnp.int32, block_map.shape, 1)
    first = jnp.min(jnp.where(here, spot, rows), axis=1, keepdims=True)
    one = jnp.max(jnp.where(here & (spot == first), held, -1), axis=1, keepdims=True)
    two = jnp.max(jnp.where(here & (spot > first), held, -1), axis=1, keepdims=True)
    owner = lax.broadcasted_iota(jnp.int32, (owners, rows), 0)
    slot = lax.broadcasted_iota(jnp.int32, (owners, rows), 1)
    place_of = jnp.where(one == slot, 2 * owner, 0) + jnp.where(two == slot, 2 * owner + 1, 0)
    return jnp.sum(place_of, axis=0, keepdims=True)


def pack_kernel(rows, chunks, map_ref, mscale_ref, sscale_ref, master_ref, mean_ref, square_ref, out_ref, *scratch):
    held_map, master, mean, square, wide_mean, wide_square, slots, mscale, sscale, slot_of, mscale_of, sscale_of = scratch[:12]
    load_sems, table_sems = scratch[12:]
    part = rows * chunks // 2
    pairs = [(map_ref, held_map)]
    for h in range(2):
        here = pl.ds(h * part, part)
        pairs += [(ref.at[here], room.at[here]) for ref, room in ((mean_ref, mean), (square_ref, square), (master_ref, master))]
    loads = [pltpu.make_async_copy(ref, room, load_sems.at[k]) for k, (ref, room) in enumerate(pairs)]
    for load in loads:
        load.start()
    mscale[...] = mscale_ref[...].astype(jnp.float32)
    sscale[...] = sscale_ref[...].astype(jnp.float32)
    loads[0].wait()
    slots[...] = send_slots(held_map[...], rows)
    tables = [(slots, slot_of), (mscale, mscale_of), (sscale, sscale_of)]
    tables = [pltpu.make_async_copy(table, room, table_sems.at[k]) for k, (table, room) in enumerate(tables)]
    for table in tables:
        table.start()
    for row in range(rows):
        if row % (rows // 2) == 0:
            first = 1 + 3 * (row * 2 // rows)
            here = pl.ds(row * chunks, part)
            loads[first].wait()
            wide_mean[here, :] = mean[here, :].astype(jnp.float32)
            loads[first + 1].wait()
            wide_square[here, :] = square[here, :].astype(jnp.float32)
            loads[first + 2].wait()
        if row == 0:
            for table in tables:
                table.wait()
        base = (row // SUB) * chunks * SUB + row % SUB
        spots = pl.ds(base, chunks, stride=SUB)
        slot = slot_of[0, row]
        out_ref[slot, pl.ds(0, chunks), :] = master[spots, :].astype(jnp.bfloat16)
        out_ref[slot, pl.ds(chunks, chunks), :] = (wide_mean[spots, :] * mscale_of[0, row]).astype(jnp.bfloat16)
        out_ref[slot, pl.ds(2 * chunks, chunks), :] = (wide_square[spots, :] * sscale_of[0, row]).astype(jnp.bfloat16)


def pack(old_map, mean_scale, square_scale, master, mean, square, slot_total):
    rows, cols = master.shape
    chunks = cols // LANES
    hbm = pl.BlockSpec(memory_space=pl.ANY)
    vmem = pl.BlockSpec(memory_space=pltpu.VMEM)
    flat = (rows * chunks, LANES)
    f32, i32 = jnp.float32, jnp.int32
    block_map = old_map.reshape(-1, rows)
    return pl.pallas_call(
        functools.partial(pack_kernel, rows, chunks),
        out_shape=jax.ShapeDtypeStruct((slot_total, 3 * chunks, LANES), jnp.bfloat16),
        in_specs=[hbm, vmem, vmem, hbm, hbm, hbm],
        out_specs=vmem,
        scratch_shapes=[
            pltpu.VMEM(block_map.shape, i32),
            pltpu.VMEM(flat, f32),
            pltpu.VMEM(flat, mean.dtype),
            pltpu.VMEM(flat, square.dtype),
            pltpu.VMEM(flat, f32),
            pltpu.VMEM(flat, f32),
            pltpu.VMEM((1, rows), i32),
            pltpu.VMEM((1, rows), f32),
            pltpu.VMEM((1, rows), f32),
            pltpu.SMEM((1, rows), i32),
            pltpu.SMEM((1, rows), f32),
            pltpu.SMEM((1, rows), f32),
            pltpu.SemaphoreType.DMA((7,)),
            pltpu.SemaphoreType.DMA((3,)),
        ],
        compiler_params=pltpu.CompilerParams(vmem_limit_bytes=56 * 1024 * 1024),
        name="pack",
    )(
        block_map,
        mean_scale.reshape(1, rows),
        square_scale.reshape(1, rows),
        to_tiles(master),
        to_tiles(mean),
        to_tiles(square),
    )


def unpack_kernel(rows, chunks, slot_ref, in_ref, out_ref, weight_old, mean_old, square_old):
    span = chunks * SUB
    stages = (weight_old, mean_old, square_old)
    for group in range(rows // SUB):
        buf = group % 2
        for r in range(SUB):
            slot = slot_ref[group * SUB + r]
            spots = pl.ds(buf * span + r, chunks, stride=SUB)
            for k, stage in enumerate(stages):
                stage[spots, :] = in_ref[slot, pl.ds(k * chunks, chunks), :].astype(jnp.float32)
        for k, stage in enumerate(stages):
            out_ref[k, pl.ds(group * span, span), :] = stage[pl.ds(buf * span, span), :].astype(out_ref.dtype)


def unpack(slots, arrived, rows, chunks):
    stage = pltpu.VMEM((2 * chunks * SUB, LANES), jnp.float32)
    vmem = pl.BlockSpec(memory_space=pltpu.VMEM)
    return pl.pallas_call(
        functools.partial(unpack_kernel, rows, chunks),
        out_shape=jax.ShapeDtypeStruct((3, rows * chunks, LANES), arrived.dtype),
        in_specs=[pl.BlockSpec(memory_space=pltpu.SMEM), vmem],
        out_specs=vmem,
        scratch_shapes=[stage, stage, stage],
        compiler_params=pltpu.CompilerParams(vmem_limit_bytes=24 * 1024 * 1024),
        name="unpack",
    )(slots, arrived)


def start_loads(half, old_ref, mine_ref, side_refs, old, addends, sems):
    loads = []
    for h in range(2):
        part = pl.ds(h * half, half)
        pairs = [(mine_ref.at[part], addends.at[0, part])]
        pairs += [(side_refs[2 * k + h], addends.at[1 + k, part]) for k in range(2)]
        pairs += [(old_ref.at[k, part], old.at[k, part]) for k in range(3)]
        loads.append([pltpu.make_async_copy(ref, room, sems.at[h, k]) for k, (ref, room) in enumerate(pairs)])
    for load in loads[0] + loads[1]:
        load.start()
    return loads


def step_values(old, gradient):
    weight_old, mean_old, square_old = (x.astype(jnp.float32) for x in old)
    mean_next = 0.9 * mean_old + 0.1 * gradient
    square_next = 0.95 * square_old + 0.05 * gradient * gradient
    root = square_next * lax.rsqrt(square_next)
    master = weight_old - 0.05 * (mean_next / (root + 1e-08) + 0.1 * weight_old)
    return mean_next, square_next, master


def weights_kernel(old_ref, mine_ref, *refs):
    side_refs, out_refs = refs[:4], refs[4:]
    half = out_refs[0].shape[0]
    for h in range(2):
        for start in range(0, half, STRIP):
            there, inside = pl.ds(h * half + start, STRIP), pl.ds(start, STRIP)
            gradient = mine_ref[there, :].astype(jnp.float32)
            for side in range(2):
                gradient += side_refs[2 * side + h][inside, :].astype(jnp.float32)
            master = step_values([old_ref[k, there, :] for k in range(3)], gradient)[2]
            out_refs[h][inside, :] = master.astype(out_refs[h].dtype)


def new_weights(old, addends, rows, chunks):
    vmem = pl.BlockSpec(memory_space=pltpu.VMEM)
    return pl.pallas_call(
        weights_kernel,
        out_shape=[jax.ShapeDtypeStruct((rows * chunks // 2, LANES), jnp.bfloat16)] * 2,
        in_specs=[vmem] * 6,
        out_specs=[vmem] * 2,
        compiler_params=pltpu.CompilerParams(vmem_limit_bytes=12 * 1024 * 1024),
        name="new_weights",
    )(old, *addends)


def adam_kernel(rows, chunks, old_ref, mine_ref, *refs):
    side_refs, weight_refs, refs = refs[:4], refs[4:6], refs[6:]
    whole_ref, master_ref, mcode_ref, scode_ref, mscale_ref, sscale_ref = refs[:6]
    old, addends, weights, sems, in_sems, out_sems = refs[6:]
    span = chunks * SUB
    groups = rows // SUB
    half = groups // 2 * span
    loads = start_loads(half, old_ref, mine_ref, side_refs, old, addends, sems)
    own = lax.axis_index("dp") * 2 * half
    fetches = [pltpu.make_async_copy(weight_refs[h], weights.at[h], in_sems.at[h]) for h in range(2)]
    stores = [
        pltpu.make_async_copy(weights.at[h], whole_ref.at[pl.ds(pl.multiple_of(own + h * half, half), half)], out_sems.at[h])
        for h in range(2)
    ]
    for fetch in fetches:
        fetch.start()
    lane = lax.broadcasted_iota(jnp.int32, (SUB, LANES), 1)
    sub = lax.broadcasted_iota(jnp.int32, (SUB, LANES), 0)
    mline = jnp.zeros((SUB, LANES), jnp.float32)
    sline = jnp.zeros((SUB, LANES), jnp.float32)
    for group in range(groups):
        if group % (groups // 2) == 0:
            h = group * 2 // groups
            for load in loads[h]:
                load.wait()
            fetches[h].wait()
            stores[h].start()
        there = pl.ds(group * span, span)
        gradient = addends[0, there, :].astype(jnp.float32)
        for k in range(1, ADDENDS):
            gradient += addends[k, there, :].astype(jnp.float32)
        mean_next, square_next, master = step_values([old[k, there, :] for k in range(3)], gradient)
        master_ref[there, :] = master
        mean_next = mean_next.reshape(chunks, SUB, LANES)
        square_next = square_next.reshape(chunks, SUB, LANES)
        mpeak = jnp.max(jnp.max(jnp.abs(mean_next), axis=0), axis=1, keepdims=True)
        speak = jnp.max(jnp.max(square_next, axis=0), axis=1, keepdims=True)
        mscale = (mpeak + 1e-06).astype(jnp.bfloat16).astype(jnp.float32)
        sscale = (speak + 1e-06).astype(jnp.bfloat16).astype(jnp.float32)
        mcode_ref[there, :] = (mean_next * (1.0 / mscale)[None]).reshape(span, LANES).astype(jnp.bfloat16)
        scode_ref[there, :] = (square_next * (1.0 / sscale)[None]).reshape(span, LANES).astype(jnp.bfloat16)
        mine = lane == sub + group * SUB
        mline = jnp.where(mine, mscale, mline)
        sline = jnp.where(mine, sscale, sline)
    mscale_ref[...] = jnp.sum(mline, axis=0, keepdims=True).astype(jnp.bfloat16)
    sscale_ref[...] = jnp.sum(sline, axis=0, keepdims=True).astype(jnp.bfloat16)
    for store in stores:
        store.wait()


def adam(old, addends, weights, rows, chunks):
    flat = (rows * chunks, LANES)
    bf16, f32 = jnp.bfloat16, jnp.float32
    vmem = pl.BlockSpec(memory_space=pltpu.VMEM)
    return pl.pallas_call(
        functools.partial(adam_kernel, rows, chunks),
        out_shape=[
            jax.ShapeDtypeStruct((RING * CORES * flat[0], LANES), bf16),
            jax.ShapeDtypeStruct(flat, f32),
            jax.ShapeDtypeStruct(flat, bf16),
            jax.ShapeDtypeStruct(flat, bf16),
            jax.ShapeDtypeStruct((1, rows), bf16),
            jax.ShapeDtypeStruct((1, rows), bf16),
        ],
        in_specs=[pl.BlockSpec(memory_space=pl.ANY)] * 8,
        out_specs=[pl.BlockSpec(memory_space=pl.ANY)] + [vmem] * 5,
        scratch_shapes=[
            pltpu.VMEM((3, *flat), bf16),
            pltpu.VMEM((ADDENDS, *flat), bf16),
            pltpu.VMEM((2, flat[0] // 2, LANES), bf16),
            pltpu.SemaphoreType.DMA((2, 3 + ADDENDS)),
            pltpu.SemaphoreType.DMA((2,)),
            pltpu.SemaphoreType.DMA((2,)),
        ],
        compiler_params=pltpu.CompilerParams(vmem_limit_bytes=56 * 1024 * 1024),
        cost_estimate=pl.CostEstimate(flops=0, transcendentals=0, bytes_accessed=16 * 1024 * 1024),
        name="adam",
    )(old, *addends, *weights)


def place():
    me = lax.axis_index("dp")
    return me // CORES, me % CORES


def shard_at(y, step, core):
    return lax.rem(y + step, RING) * CORES + core


def sends(shift, flip):
    return [
        (y * CORES + c, (y + shift) % RING * CORES + (CORES - 1 - c if flip else c))
        for y in range(RING)
        for c in range(CORES)
    ]


def send(values, shift, flip=False, name="r_send"):
    with jax.named_scope(name):
        return lax.ppermute(values, "dp", sends(shift, flip))


def cut_kernel(shards, grad_ref, *refs):
    out_refs, (room, in_sems, out_sems) = refs[: len(shards)], refs[len(shards) :]
    y, core = place()
    loads, stores = [], []
    for k, (step, flip) in enumerate(shards):
        shard = shard_at(y, step, CORES - 1 - core if flip else core)
        loads.append(pltpu.make_async_copy(grad_ref.at[shard], room.at[k], in_sems.at[k]))
        stores.append(pltpu.make_async_copy(room.at[k], out_refs[k], out_sems.at[k]))
    for load in loads:
        load.start()
    for load, store in zip(loads, stores):
        load.wait()
        store.start()
    for store in stores:
        store.wait()


def cut(grads, shards):
    _, span, lanes = grads.shape
    count = len(shards)
    hbm = pl.BlockSpec(memory_space=pl.ANY)
    return pl.pallas_call(
        functools.partial(cut_kernel, shards),
        out_shape=[jax.ShapeDtypeStruct((span, lanes), grads.dtype)] * count,
        in_specs=[hbm],
        out_specs=[hbm] * count,
        scratch_shapes=[pltpu.VMEM((count, span, lanes), grads.dtype)] + [pltpu.SemaphoreType.DMA((count,))] * 2,
        compiler_params=pltpu.CompilerParams(vmem_limit_bytes=56 * 1024 * 1024),
        name="cut",
    )(grads)


def add_kernel(windows, sums, *refs):
    count, outs = len(windows), len(sums)
    in_refs, out_refs, rooms, totals = refs[:count], refs[count:][:outs], refs[count + outs :][:count], refs[2 * count + outs : -2]
    in_sems, out_sems = refs[-2:]
    loads = [
        pltpu.make_async_copy(ref.at[pl.ds(*window)], room, in_sems.at[k])
        for k, (ref, window, room) in enumerate(zip(in_refs, windows, rooms))
    ]
    for load in loads:
        load.start()
    stores = []
    for k, terms in enumerate(sums):
        total = None
        for term in terms:
            loads[term].wait()
            values = rooms[term][...].astype(jnp.float32)
            total = values if total is None else total + values
        totals[k][...] = total.astype(totals[k].dtype)
        store = pltpu.make_async_copy(totals[k], out_refs[k], out_sems.at[k])
        store.start()
        stores.append(store)
    for store in stores:
        store.wait()


def add(*sums):
    terms = [term for parts in sums for term in parts]
    lanes, dtype = terms[0][0].shape[1], terms[0][0].dtype
    hbm = pl.BlockSpec(memory_space=pl.ANY)
    order, at = [], 0
    for parts in sums:
        order.append(tuple(range(at, at + len(parts))))
        at += len(parts)
    windows = [(first, rows) for _, first, rows in terms]
    shapes = [(rows, lanes) for _, rows in windows]
    outs = [(parts[0][2], lanes) for parts in sums]
    return pl.pallas_call(
        functools.partial(add_kernel, windows, order),
        out_shape=[jax.ShapeDtypeStruct(shape, dtype) for shape in outs],
        in_specs=[hbm] * len(terms),
        out_specs=[hbm] * len(outs),
        scratch_shapes=[pltpu.VMEM(shape, dtype) for shape in shapes + outs]
        + [pltpu.SemaphoreType.DMA((len(terms),)), pltpu.SemaphoreType.DMA((len(outs),))],
        compiler_params=pltpu.CompilerParams(vmem_limit_bytes=56 * 1024 * 1024),
        name="add",
    )(*[array for array, _, _ in terms])


def reduce_shards(grads, arrived):
    span = grads.shape[1]
    half = span // 2
    steps = (2, 1, 3, 0)
    got = dict(zip(steps, [send(part, 0, True) for part in cut(grads, tuple((step, 1) for step in steps))]))
    own = dict(zip(steps, cut(grads, tuple((step, 0) for step in steps))))

    def both(step, first, rows):
        return [(own[step], first, rows), (got[step], first, rows)]

    opp_lo, opp_hi, up_hi, dn_lo, up_lo, dn_hi, mine = add(
        both(2, 0, half),
        both(2, half, half),
        both(1, half, half),
        both(3, 0, half),
        both(1, 0, half),
        both(3, half, half),
        both(0, 0, span),
    )
    opp_up, opp_dn = send(opp_lo, 1), send(opp_hi, 3)
    up_hi_got, dn_lo_got = send(up_hi, 1), send(dn_lo, 3)
    opp_up, opp_dn, arrived = lax.optimization_barrier((opp_up, opp_dn, arrived))
    up_lo, dn_hi = add([(up_lo, 0, half), (opp_up, 0, half)], [(dn_hi, 0, half), (opp_dn, 0, half)])
    return (mine, send(up_lo, 1), up_hi_got, dn_lo_got, send(dn_hi, 3)), arrived


def join_kernel(span, starts, *refs):
    parts, (out_ref, sems) = refs[: len(starts)], refs[-2:]
    y, core = place()
    copies = []
    for k, (step, flip, offset) in enumerate(starts):
        side = CORES - 1 - core if flip else core
        base = pl.multiple_of(shard_at(y, step, side) * span + offset, span // 2)
        copies.append(pltpu.make_async_copy(parts[k], out_ref.at[pl.ds(base, parts[k].shape[0])], sems.at[k]))
    for copy in copies:
        copy.start()
    for copy in copies:
        copy.wait()


def join(span, starts, parts, whole):
    return pl.pallas_call(
        functools.partial(join_kernel, span, starts),
        out_shape=jax.ShapeDtypeStruct(whole.shape, whole.dtype),
        in_specs=[pl.BlockSpec(memory_space=pltpu.VMEM)] * len(parts) + [pl.BlockSpec(memory_space=pl.ANY)],
        out_specs=pl.BlockSpec(memory_space=pl.ANY),
        scratch_shapes=[pltpu.SemaphoreType.DMA((len(parts),))],
        compiler_params=pltpu.CompilerParams(vmem_limit_bytes=8 * 1024 * 1024),
        input_output_aliases={len(parts): 0},
        name="join",
    )(*parts, whole)


def gather_shards(lo, hi, run_between):
    half = lo.shape[0]
    span = 2 * half
    up_lo, dn_hi = send(lo, 1, name="g_up_lo"), send(hi, 3, name="g_dn_hi")
    up_hi, dn_lo = send(hi, 1, name="g_up_hi"), send(lo, 3, name="g_dn_lo")
    sib_lo, sib_hi = send(lo, 0, True, name="g_sib_lo"), send(hi, 0, True, name="g_sib_hi")
    whole, *rest = run_between(sib_lo)
    up_lo, dn_hi, rest[-1] = lax.optimization_barrier((up_lo, dn_hi, rest[-1]))
    opp_lo, opp_hi = send(up_lo, 1, name="g_opp_lo"), send(dn_hi, 3, name="g_opp_hi")
    sib_up_lo, sib_dn_hi = send(up_lo, 0, True, name="g_sib_up_lo"), send(dn_hi, 0, True, name="g_sib_dn_hi")
    starts = [(3, 0, 0), (1, 0, half), (3, 0, half), (1, 0, 0), (0, 1, 0), (0, 1, half)]
    whole = join(span, starts, [up_lo, dn_hi, up_hi, dn_lo, sib_lo, sib_hi], whole)
    whole, up_hi, dn_lo, opp_lo, opp_hi = lax.optimization_barrier((whole, up_hi, dn_lo, opp_lo, opp_hi))
    parts = [opp_lo, opp_hi]
    for part, name in zip((opp_lo, opp_hi, up_hi, dn_lo), ("opp_lo", "opp_hi", "up_hi", "dn_lo")):
        parts.append(send(part, 0, True, name="g_sib_" + name))
    parts += [sib_up_lo, sib_dn_hi]
    starts = [(2, 0, 0), (2, 0, half), (2, 1, 0), (2, 1, half), (3, 1, half), (1, 1, 0), (3, 1, 0), (1, 1, half)]
    late = [k for k in range(len(parts)) if k in (2, 3)]
    soon = [k for k in range(len(parts)) if k not in late]
    whole = join(span, [starts[k] for k in soon], [parts[k] for k in soon], whole)
    return join(span, [starts[k] for k in late], [parts[k] for k in late], whole), rest


def arrivals(old_map, block_rows, peer_cap):
    self_index = lax.axis_index(ALL)
    wanted = lax.dynamic_slice_in_dim(old_map, self_index * block_rows, block_rows)
    source = wanted // block_rows
    return source * peer_cap + pair_rank(source, jnp.arange(block_rows, dtype=jnp.int32))


def local(grad_parts, old_master, old_mean, old_mean_scale, old_square, old_square_scale, old_map):
    count_all = lax.axis_size(ALL)
    block_rows, block_len = old_master.shape
    peer_cap = 2
    slot_total = count_all * peer_cap
    chunks = block_len // LANES
    grads = to_tiles(grad_parts[0]).reshape(RING * CORES, block_rows * chunks, LANES)
    packed = pack(old_map, old_mean_scale, old_square_scale, old_master, old_mean, old_square, slot_total)
    packed, late_grads, late_map = lax.optimization_barrier((packed, grads, old_map))
    arrived = lax.all_to_all(
        packed.reshape(count_all, peer_cap * 3 * chunks, LANES), ALL, split_axis=0, concat_axis=0, tiled=True
    ).reshape(slot_total, 3 * chunks, LANES)
    addends, arrived = reduce_shards(late_grads, arrived)
    old = unpack(arrivals(late_map, block_rows, peer_cap), arrived, block_rows, chunks)
    lo, hi = new_weights(old, addends, block_rows, chunks)

    def run_between(*arrived_first):
        late_old, late_addends, _ = lax.optimization_barrier((old, addends, arrived_first))
        return adam(late_old, late_addends, (lo, hi), block_rows, chunks)

    weights, rest = gather_shards(lo, hi, run_between)
    *blocks, mean_scales, square_scales = rest
    master, mean_codes, square_codes = (from_tiles(x, block_rows, block_len) for x in blocks)
    weights = from_tiles(weights, RING * CORES * block_rows, block_len)
    return (weights, master, mean_codes, mean_scales.reshape(-1), square_codes, square_scales.reshape(-1))


def solution(mesh):
    in_specs = (
        P("dp", "fsdp", None),
        P(ALL, None),
        P(ALL, None),
        P(ALL),
        P(ALL, None),
        P(ALL),
        P(),
    )
    out_specs = (
        P("fsdp", None),
        P(ALL, None),
        P(ALL, None),
        P(ALL),
        P(ALL, None),
        P(ALL),
    )
    return jax.shard_map(local, mesh=mesh, in_specs=in_specs, out_specs=out_specs, check_vma=False)
```
